128 devices in a mesh: tiles: 16 (over y, z), nests: 8 (over x, core).
Axes of the slice: x: 4, y: 4, z: 4, core: 2. Of those that a mesh axis runs over, the one named last changes fastest.
Arguments:
- parent: float32 [1024, 2048, 128], P('tiles', 'nests'), may hold values from -6 to 6
- nest_state: float32 [8, 64, 128, 128], P('nests', 'tiles'), may hold values from -6 to 6
- parent_mix: float32 [128, 128], replicated, may hold values from -0.24 to 0.24
- nest_mix: float32 [128, 128], replicated, may hold values from -0.24 to 0.24
- courant: float32 [2, 128], replicated, may hold values from 0.05 to 0.45
- nest_pos: int32 [8, 2], P('nests'), may hold values from 0 to 5954, as said below
Outputs:
- parent_out: float32 [1024, 2048, 128], P('tiles', 'nests')
- nest_out: float32 [8, 64, 128, 128], P('nests', 'tiles')
The draws below stay inside these ranges and needn't reach their ends.
Inputs may be any that keep to these rules, and one draw needn't show every extreme that they name: nest_pos[n] = (3 i + a, 3 q + c) with a, c in 0..2, i <= 1001, and n * 256 <= q <= (n + 1) * 256 - 64: nest n reads and feeds only parent columns of the n-th group of 256 columns.
All inputs are finite; a program needn't handle non-finite values.
Results may differ from the reference program's by a relative error of at most 0.0003.
Values sent between devices are 32-bit elements; how exact they have to be, the bound alone decides.
No kernel may reach another device: no remote copies, remote signals or barrier semaphores. Data moves between devices by JAX's collectives and lax.ppermute only.
A program may use at most 128 MiB of HBM per device.

```python
import jax
import jax.numpy as jnp
from jax import lax

COL = 128
TY = 256
BLK = 64
NY = 128
STEPS = 3
PX = 1024
PY = 2048
NX = 64
WIN = 24
NESTS = 8


def draw_nest_pos(key, part):
    need = (NX + 1) // 3 + 2
    start_rows = jax.random.randint(jax.random.fold_in(key, 101), (NESTS,), 0, PX - need + 1).astype(jnp.int32)
    phase_x = jax.random.randint(jax.random.fold_in(key, 102), (NESTS,), 0, 3).astype(jnp.int32)
    within = jax.random.randint(jax.random.fold_in(key, 103), (NESTS,), 0, TY - BLK + 1).astype(jnp.int32)
    phase_y = jax.random.randint(jax.random.fold_in(key, 104), (NESTS,), 0, 3).astype(jnp.int32)
    start_rows = start_rows.at[0].set(PX - need).at[1].set(0)
    phase_x = phase_x.at[0].set(2).at[1].set(0)
    within = within.at[NESTS - 1].set(TY - BLK)
    phase_y = phase_y.at[NESTS - 1].set(2)
    corner = jnp.arange(NESTS, dtype=jnp.int32) * TY + within
    return jnp.stack([3 * start_rows + phase_x, 3 * corner + phase_y], axis=1).astype(jnp.int32)


def block_levels(own_key, shape, cuts, low, top_value):
    def one(dim, parts):
        steps = jax.random.uniform(jax.random.fold_in(jax.random.fold_in(own_key, 6), dim), (parts,), jnp.float32, low / len(cuts), top_value / len(cuts))
        return jnp.repeat(jnp.exp(steps), shape[dim] // parts).reshape((-1,) + (1,) * (len(shape) - dim - 1))

    gain = one(*cuts[0])
    for cut in cuts[1:]:
        gain = gain * one(*cut)
    return gain


def centred(rng, extent, width, limit, cuts=(), kind=jnp.bfloat16):
    entries = width * jax.random.normal(rng, extent, jnp.float32)
    if cuts:
        entries = entries * block_levels(rng, extent, cuts, -0.22, 0.18)
    return jnp.clip(entries, -limit, limit).astype(kind)


def setup_inputs(seed: int = 0) -> dict:
    keys = jax.random.split(jax.random.key(seed), 7)
    return {
        "parent": centred(keys[0], (PX, PY, COL), 1.0, 6.0, ((0, 16), (1, 8)), jnp.float32),
        "nest_state": centred(keys[1], (NESTS, NX, NY, COL), 1.0, 6.0, ((0, 8), (1, 16)), jnp.float32),
        "parent_mix": centred(keys[2], (COL, COL), 0.04, 0.24, (), jnp.float32),
        "nest_mix": centred(keys[3], (COL, COL), 0.04, 0.24, (), jnp.float32),
        "courant": jnp.clip(jax.random.uniform(keys[4], (2, COL), jnp.float32, 0.05, 0.45), 0.05, 0.45),
        "nest_pos": draw_nest_pos(jax.random.fold_in(keys[6], 71), 0),
    }


KAPPA = 0.125
HIGH = lax.Precision.HIGHEST


def parent_advance(parent, parent_mix):
    padded = jnp.pad(parent, ((1, 1), (1, 1), (0, 0)))
    beside_all = padded[2:, 1:-1] + padded[:-2, 1:-1] + padded[1:-1, 2:] + padded[1:-1, :-2]
    mixed = jnp.einsum('xyc,cd->xyd', parent, parent_mix, precision=HIGH)
    return parent + KAPPA * (beside_all - 4.0 * parent) + mixed


def nest_advance(current, upper, edge, courant, nest_mix):
    left = jnp.concatenate([edge, current[:, :-1]], axis=1)
    mixed = jnp.einsum('xyc,cd->xyd', current, nest_mix, precision=HIGH)
    return current + courant[0] * (upper - current) + courant[1] * (left - current) + mixed


def bilinear(data, anchor, rows, columns_count, block_len):
    cols = jnp.arange(columns_count, dtype=jnp.int32)
    spot = anchor[1] + cols
    near = spot // 3 - anchor[1] // 3
    frac_y = (spot % 3).astype(jnp.float32) / 3.0
    places = jnp.arange(block_len, dtype=jnp.int32)[None, :]
    zero = jnp.zeros((columns_count, block_len), jnp.float32)
    table = jnp.where(places == near[:, None], (1.0 - frac_y)[:, None] + zero, zero)
    table = table + jnp.where(places == near[:, None] + 1, frac_y[:, None] + zero, zero)
    frac_x = ((anchor[0] + rows) % 3).astype(jnp.float32) / 3.0
    upper_part = jnp.einsum('nb,xbc->xnc', table, data[:, 0], precision=HIGH)
    lower_part = jnp.einsum('nb,xbc->xnc', table, data[:, 1], precision=HIGH)
    return (1.0 - frac_x)[:, None, None] * upper_part + frac_x[:, None, None] * lower_part


def reference(parent, nest_state, parent_mix, nest_mix, courant, nest_pos):
    padded_rows = jnp.concatenate([parent, jnp.zeros((WIN, PY, COL), parent.dtype)], axis=0)
    naught = jnp.zeros((), jnp.int32)

    def one_nest(packed):
        anchor, state = packed
        top = (anchor[0] // 3).astype(jnp.int32)
        corner = (anchor[1] // 3).astype(jnp.int32)
        band = lax.dynamic_slice(padded_rows, (top, corner, naught), (WIN, BLK, COL))
        rows = jnp.arange(NX, dtype=jnp.int32)
        near_row = (anchor[0] + rows) // 3 - top
        data = jnp.stack([band[near_row], band[near_row + 1]], axis=1)
        interp = bilinear(data, anchor, rows, NY, BLK)
        start = 0.5 * (state + interp)
        edge = start[:, :1]
        current = start
        for step in range(STEPS):
            upper = jnp.concatenate([start[:1], current[:-1]], axis=0)
            current = nest_advance(current, upper, edge, courant, nest_mix)
        return current

    nest_out = lax.map(one_nest, (nest_pos, nest_state))
    parent_new = parent_advance(parent, parent_mix)

    fb_rows = (NX + 2) // 3
    fb_cols = (NY + 2) // 3
    parent_out = parent_new
    for nest_index in range(NESTS):
        anchor_x = nest_pos[nest_index, 0]
        anchor_y = nest_pos[nest_index, 1]
        xs = (-anchor_x) % 3 + 3 * jnp.arange(fb_rows, dtype=jnp.int32)
        ys = (-anchor_y) % 3 + 3 * jnp.arange(fb_cols, dtype=jnp.int32)
        valid = (xs < NX)[:, None] & (ys < NY)[None, :]
        values = nest_out[nest_index][jnp.clip(xs, 0, NX - 1)][:, jnp.clip(ys, 0, NY - 1)]
        prow = (anchor_x + xs) // 3
        pcol = (anchor_y + ys) // 3
        old = parent_new[jnp.clip(prow, 0, PX - 1)[:, None], jnp.clip(pcol, 0, PY - 1)[None, :]]
        diff = jnp.where(valid[..., None], 0.5 * (values - old), 0.0)
        row_index = jnp.where(valid, prow[:, None], PX)
        col_index = jnp.broadcast_to(pcol[None, :], valid.shape)
        parent_out = parent_out.at[row_index, col_index].add(diff, mode="drop")
    return parent_out, nest_out
```

```python
import functools

import jax
import jax.numpy as jnp
from jax import lax
from jax.experimental import pallas as pl
from jax.experimental.pallas import tpu as pltpu
from jax.sharding import PartitionSpec as P

STEPS = 3
KAPPA = 0.125
C = 48
WIDE = 56
SIDE = 4
GROUP_ROWS = 8
DEV_ROWS = 4
FB_SLOTS = 2
FB_GROUP = 6
FB_WINDOW = 22
F32 = jnp.float32
BF16 = jnp.bfloat16


def third(value):
    return lax.div(value, jnp.int32(3))


def wrap(value):
    return lax.rem(value + 2 * SIDE, jnp.int32(SIDE))


def split(value):
    high = value.astype(BF16)
    return high, (value - high.astype(F32)).astype(BF16)


def wide_weights(matrix):
    high, low = split(matrix)
    row = jnp.concatenate([high, low], axis=1)
    return jnp.concatenate([row, row], axis=0)


def mix(value, weights):
    lhs = jnp.concatenate(split(value), axis=1)
    both = jnp.dot(lhs, weights, preferred_element_type=F32)
    half = both.shape[1] // 2
    return both[:, :half] + both[:, half:]


def eye(size):
    shape = (size, size)
    return lax.broadcasted_iota(jnp.int32, shape, 0) == lax.broadcasted_iota(jnp.int32, shape, 1)


def owner_place(row, first, tile_rows):
    owner = lax.div(jnp.maximum(row, 0), jnp.int32(tile_rows))
    base = owner * tile_rows
    begin = jnp.clip(first - base, 0, tile_rows - GROUP_ROWS)
    return owner, jnp.clip(row - base - begin, 0, GROUP_ROWS - 1)


def pack_kernel(tile_rows, tile_cols, nest_rows, pos, parent, nest, b0, b1, b2, b3, west, east, down, up, band, cols, sems):
    tile = lax.axis_index("tiles")
    line = lax.axis_index("nests")
    my_y = lax.div(tile, jnp.int32(SIDE))
    corner = third(pos[0, 1]) - line * tile_cols
    aligned = pl.multiple_of(lax.div(corner, jnp.int32(8)) * 8, 8)
    shift = corner - aligned
    copies = []
    for k in range(SIDE):
        group = wrap(my_y + k)
        first = third(pos[0, 0] + SIDE * nest_rows * group) - 1
        begin = jnp.clip(first - tile * tile_rows, 0, tile_rows - GROUP_ROWS)
        copies.append(
            pltpu.make_async_copy(
                parent.at[pl.ds(begin, GROUP_ROWS), pl.ds(aligned, WIDE)], band.at[k], sems.at[k]
            )
        )
    halo = 3
    others = [
        pltpu.make_async_copy(parent.at[:, pl.ds(0, 8)], cols.at[0], sems.at[4]),
        pltpu.make_async_copy(parent.at[:, pl.ds(tile_cols - 8, 8)], cols.at[1], sems.at[5]),
        pltpu.make_async_copy(parent.at[tile_rows - 1], down.at[pl.ds(0, tile_cols)], sems.at[6]),
        pltpu.make_async_copy(parent.at[0], up, sems.at[7]),
    ]
    nest_cols = nest.shape[1]
    for r in range(halo):
        others.append(
            pltpu.make_async_copy(
                nest.at[nest_rows - halo + r],
                down.at[pl.ds(tile_cols + r * nest_cols, nest_cols)],
                sems.at[8 + r],
            )
        )
    for copy in copies + others:
        copy.start()
    for k, out in enumerate((b0, b1, b2, b3)):
        copies[k].wait()
        for r in range(GROUP_ROWS):
            out[r] = band[k, r, pl.ds(shift, C), :]
    others[0].wait()
    west[...] = cols[0, :, 0, :]
    others[1].wait()
    east[...] = cols[1, :, 7, :]
    for copy in others[2:]:
        copy.wait()


def pick_kernel(tile_rows, nest_rows, pos, r0, r1, r2, r3, o0, o1, o2, o3):
    tile = lax.axis_index("tiles")
    my_y, my_z = lax.div(tile, jnp.int32(SIDE)), lax.rem(tile, jnp.int32(SIDE))
    first = third(pos[0, 0] + SIDE * nest_rows * my_y) - 1
    for k, out in enumerate((o0, o1, o2, o3)):
        target = my_y * SIDE + wrap(my_z + k)
        top = third(pos[0, 0] + nest_rows * target) - 1
        for j in range(DEV_ROWS):
            owner, place = owner_place(top + j, first, tile_rows)
            way = wrap(my_y - lax.div(owner, jnp.int32(SIDE)))
            for source, ref in enumerate((r0, r1, r2, r3)):

                @pl.when(way == source)
                def _(out=out, j=j, ref=ref, place=place):
                    out[j] = ref[place]


def nest_kernel(tile_rows, tile_cols, pos, r0, r1, r2, r3, state, down, nest_mix, courant, out, fb, lines, start, cur):
    tile = lax.axis_index("tiles")
    my_y, my_z = lax.div(tile, jnp.int32(SIDE)), lax.rem(tile, jnp.int32(SIDE))
    nest_rows, ncols, width = state.shape
    halo = STEPS
    ox, oy = pos[0, 0], pos[0, 1]
    phase = lax.rem(oy, jnp.int32(3))
    top = third(ox + nest_rows * tile) - 1
    spot = lax.broadcasted_iota(jnp.int32, (ncols, C), 0) + phase
    near = third(spot)
    frac = spot - 3 * near
    place = lax.broadcasted_iota(jnp.int32, (ncols, C), 1)
    table = jnp.where(place == near, 3 - frac, jnp.where(place == near + 1, frac, 0))
    table = table.astype(F32).astype(BF16)
    for j in range(DEV_ROWS):
        owner = lax.div(jnp.maximum(top + j, 0), jnp.int32(tile_rows))
        way = wrap(my_z - lax.rem(owner, jnp.int32(SIDE)))
        row = jnp.where(way == 0, r0[j], jnp.where(way == 1, r1[j], jnp.where(way == 2, r2[j], r3[j])))
        high, low = split(row)
        lines[j] = jnp.dot(table, high, preferred_element_type=F32) + jnp.dot(
            table, low, preferred_element_type=F32
        )
    for x in range(-halo, nest_rows):
        at = ox + nest_rows * tile + x
        at = jnp.maximum(at, 0)
        near_row = jnp.clip(third(at) - top, 0, DEV_ROWS - 2)
        part = lax.rem(at, jnp.int32(3)).astype(F32)
        interp = (3.0 - part) * lines[near_row] + part * lines[near_row + 1]
        own = state[x] if x >= 0 else down[pl.ds(tile_cols + (x + halo) * ncols, ncols), :]
        start[x + halo] = 0.5 * (own + interp * (1.0 / 9.0))
    first = tile == 0

    @pl.when(first)
    def _():
        for x in range(halo):
            start[x] = start[halo]

    c0, c1 = courant[0:1, :], courant[1:2, :]
    weights = wide_weights(nest_mix[...] + jnp.where(eye(width), 1.0 - c0 - c1, 0.0))
    edge_row = lax.broadcasted_iota(jnp.int32, (ncols, width), 0) == 0
    source = start
    for step in range(STEPS):
        last = step == STEPS - 1
        for r in range(nest_rows + halo - 1, step, -1):
            value = source[r]
            left = jnp.where(edge_row, start[r, 0:1, :], pltpu.roll(value, 1, 0))
            value = mix(value, weights) + c0 * source[r - 1] + c1 * left
            if r < halo:
                value = jnp.where(first, start[halo], value)
            if last:
                out[r - halo] = value
            else:
                cur[step, r] = value
        source = cur.at[step]
    rem_y = lax.rem(3 - phase, jnp.int32(3))
    slot = lax.broadcasted_iota(jnp.int32, (C, ncols), 0)
    choose = (lax.broadcasted_iota(jnp.int32, (C, ncols), 1) == rem_y + 3 * slot).astype(F32).astype(BF16)
    x0 = lax.rem(3 * nest_rows * SIDE * SIDE - lax.rem(ox + nest_rows * tile, jnp.int32(3)), jnp.int32(3))
    for s in range(FB_SLOTS):
        high, low = split(out[jnp.minimum(x0 + 3 * s, nest_rows - 1)])
        fb[s] = jnp.dot(choose, high, preferred_element_type=F32) + jnp.dot(
            choose, low, preferred_element_type=F32
        )


def up_third(value):
    return third(value + 2)


def combine_kernel(nest_rows, pos, e0, e1, e2, e3, out):
    tile = lax.axis_index("tiles")
    my_y, my_z = lax.div(tile, jnp.int32(SIDE)), lax.rem(tile, jnp.int32(SIDE))
    ox = pos[0, 0]
    base = up_third(ox + SIDE * nest_rows * my_y)
    for r in range(FB_GROUP):
        out[r] = jnp.zeros(out.shape[1:], F32)
    for k, ref in enumerate((e0, e1, e2, e3)):
        origin = ox + nest_rows * (SIDE * my_y + wrap(my_z - k))
        row = up_third(origin)
        for s in range(FB_SLOTS):

            @pl.when(3 * (row + s) - origin < nest_rows)
            def _(ref=ref, row=row, s=s):
                out[row + s - base] = ref[s]


def patch_kernel(tile_rows, tile_cols, nest_rows, ncols, pos, parent, g0, g1, g2, g3, out, buf, sems):
    tile = lax.axis_index("tiles")
    line = lax.axis_index("nests")
    my_y = lax.div(tile, jnp.int32(SIDE))
    ox, oy = pos[0, 0], pos[0, 1]
    total = nest_rows * SIDE * SIDE
    low_row = up_third(ox)
    high_row = third(ox + total - 1)
    first_row = tile * tile_rows

    @pl.when((high_row >= first_row) & (low_row < first_row + tile_rows))
    def _():
        begin = jnp.clip(low_row - first_row, 0, tile_rows - FB_WINDOW)
        corner = up_third(oy) - line * tile_cols
        aligned = pl.multiple_of(lax.div(corner, jnp.int32(8)) * 8, 8)
        shift = corner - aligned
        rem_y = 3 * up_third(oy) - oy
        place = (pl.ds(begin, FB_WINDOW), pl.ds(aligned, WIDE))
        copy = pltpu.make_async_copy(parent.at[place], buf, sems.at[0])
        copy.start()
        copy.wait()
        live = rem_y + 3 * lax.broadcasted_iota(jnp.int32, (C, buf.shape[2]), 0) < ncols

        @pl.loop(0, FB_WINDOW)
        def _(j):
            row = first_row + begin + j
            x = 3 * row - ox

            @pl.when((x >= 0) & (x < total))
            def _():
                group = lax.div(x, jnp.int32(SIDE * nest_rows))
                way = wrap(my_y - group)
                r = row - up_third(ox + SIDE * nest_rows * group)
                value = jnp.where(way == 0, g0[r], jnp.where(way == 1, g1[r], jnp.where(way == 2, g2[r], g3[r])))
                old = buf[j, pl.ds(shift, C), :]
                buf[j, pl.ds(shift, C), :] = jnp.where(live, 0.5 * (old + value), old)

        back = pltpu.make_async_copy(buf, out.at[place], sems.at[1])
        back.start()
        back.wait()


def parent_kernel(rows, main, above, below, from_up, from_down, west, east, parent_mix, out, weights):
    step = pl.program_id(0)
    count = pl.num_programs(0)

    @pl.when(step == 0)
    def _():
        size = parent_mix.shape[0]
        weights[...] = wide_weights(parent_mix[...] + jnp.where(eye(size), 1.0 - 4.0 * KAPPA, 0.0))

    cols = main.shape[1]
    index = lax.broadcasted_iota(jnp.int32, main.shape[1:], 0)
    low_edge, high_edge = index == 0, index == cols - 1
    for r in range(rows):
        value = main[r]
        upper = jnp.where(step == 0, from_up[...], above[0]) if r == 0 else main[r - 1]
        lower = jnp.where(step == count - 1, from_down[...], below[0]) if r == rows - 1 else main[r + 1]
        left = jnp.where(low_edge, west[r : r + 1, :], pltpu.roll(value, 1, 0))
        right = jnp.where(high_edge, east[r : r + 1, :], pltpu.roll(value, cols - 1, 0))
        out[r] = mix(value, weights[...]) + KAPPA * ((upper + lower) + (left + right))


def smem():
    return pl.BlockSpec(memory_space=pltpu.SMEM)


def vmem():
    return pl.BlockSpec(memory_space=pltpu.VMEM)


def hbm():
    return pl.BlockSpec(memory_space=pl.ANY)


def send(block, axis, route):
    return lax.ppermute(block, axis, route)


def y_route(k):
    return [(t, (t + SIDE * k) % (SIDE * SIDE)) for t in range(SIDE * SIDE)]


def z_route(k):
    return [(t, t // SIDE * SIDE + (t + k) % SIDE) for t in range(SIDE * SIDE)]


def shards(parent, nest_state, parent_mix, nest_mix, courant, nest_pos):
    tile_rows, tile_cols, width = parent.shape
    state = nest_state[0]
    nest_rows, ncols, _ = state.shape
    f = lambda *shape: jax.ShapeDtypeStruct(shape, F32)
    limit = pltpu.CompilerParams(vmem_limit_bytes=40 << 20)

    band = [f(GROUP_ROWS, C, width)] * SIDE
    packed = pl.pallas_call(
        functools.partial(pack_kernel, tile_rows, tile_cols, nest_rows),
        out_shape=band
        + [f(tile_rows, width)] * 2
        + [f(tile_cols + STEPS * ncols, width), f(tile_cols, width)],
        in_specs=[smem(), hbm(), hbm()],
        out_specs=[vmem()] * 6 + [hbm()] * 2,
        scratch_shapes=[
            pltpu.VMEM((SIDE, GROUP_ROWS, WIDE, width), F32),
            pltpu.VMEM((2, tile_rows, 8, width), F32),
            pltpu.SemaphoreType.DMA((11,)),
        ],
        compiler_params=limit,
        name="pack",
    )(nest_pos, parent, state)
    b, (west_out, east_out, down_out, up_out) = packed[:4], packed[4:]
    got = [b[0]] + [send(b[k], "tiles", y_route(k)) for k in range(1, SIDE)]

    count = SIDE * SIDE
    forward = [(i, i + 1) for i in range(count - 1)]
    backward = [(i + 1, i) for i in range(count - 1)]
    lines = lax.axis_size("nests")
    from_down = send(up_out, "tiles", backward)
    from_up = send(down_out, "tiles", forward)
    west = send(east_out, "nests", [(i, i + 1) for i in range(lines - 1)])
    east = send(west_out, "nests", [(i + 1, i) for i in range(lines - 1)])

    picked = pl.pallas_call(
        functools.partial(pick_kernel, tile_rows, nest_rows),
        out_shape=[f(DEV_ROWS, C, width)] * SIDE,
        in_specs=[smem()] + [vmem()] * 4,
        out_specs=[vmem()] * 4,
        name="pick",
    )(nest_pos, *got)
    mine = [picked[0]] + [send(picked[k], "tiles", z_route(k)) for k in range(1, SIDE)]

    rows = 8
    blocks = tile_rows // rows
    whole = lambda *shape: pl.BlockSpec(shape, lambda i: (0,) * len(shape))
    parent_new = pl.pallas_call(
        functools.partial(parent_kernel, rows),
        out_shape=f(tile_rows, tile_cols, width),
        grid=(blocks,),
        in_specs=[
            pl.BlockSpec((rows, tile_cols, width), lambda i: (i, 0, 0)),
            pl.BlockSpec((1, tile_cols, width), lambda i: (jnp.maximum(i * rows - 1, 0), 0, 0)),
            pl.BlockSpec((1, tile_cols, width), lambda i: (jnp.minimum(i * rows + rows, tile_rows - 1), 0, 0)),
            whole(tile_cols, width),
            whole(tile_cols, width),
            pl.BlockSpec((rows, width), lambda i: (i, 0)),
            pl.BlockSpec((rows, width), lambda i: (i, 0)),
            whole(width, width),
        ],
        out_specs=pl.BlockSpec((rows, tile_cols, width), lambda i: (i, 0, 0)),
        scratch_shapes=[pltpu.VMEM((2 * width, 2 * width), BF16)],
        compiler_params=limit,
        cost_estimate=pl.CostEstimate(flops=2 * 16384 * 256 * 256, bytes_accessed=20 << 20, transcendentals=0),
        name="parent_step",
    )(parent, parent, parent, from_up, from_down, west, east, parent_mix)

    total_rows = nest_rows + STEPS
    nest_out, fed = pl.pallas_call(
        functools.partial(nest_kernel, tile_rows, tile_cols),
        out_shape=[f(nest_rows, ncols, width), f(FB_SLOTS, C, width)],
        in_specs=[smem()] + [vmem()] * 8,
        out_specs=[vmem()] * 2,
        scratch_shapes=[
            pltpu.VMEM((DEV_ROWS, ncols, width), F32),
            pltpu.VMEM((total_rows, ncols, width), F32),
            pltpu.VMEM((STEPS - 1, total_rows, ncols, width), F32),
        ],
        compiler_params=limit,
        name="nest_steps",
    )(nest_pos, *mine, state, from_up, nest_mix, courant)

    feeds = [fed] + [send(fed, "tiles", z_route(k)) for k in range(1, SIDE)]
    joined = pl.pallas_call(
        functools.partial(combine_kernel, nest_rows),
        out_shape=f(FB_GROUP, C, width),
        in_specs=[smem()] + [vmem()] * 4,
        out_specs=vmem(),
        name="combine",
    )(nest_pos, *feeds)
    groups = [joined] + [send(joined, "tiles", y_route(k)) for k in range(1, SIDE)]
    parent_out = pl.pallas_call(
        functools.partial(patch_kernel, tile_rows, tile_cols, nest_rows, ncols),
        out_shape=f(tile_rows, tile_cols, width),
        in_specs=[smem(), hbm()] + [vmem()] * 4,
        out_specs=hbm(),
        scratch_shapes=[pltpu.VMEM((FB_WINDOW, WIDE, width), F32), pltpu.SemaphoreType.DMA((2,))],
        input_output_aliases={1: 0},
        compiler_params=limit,
        name="patch",
    )(nest_pos, parent_new, *groups)
    return parent_out, nest_out[None]


def solution(mesh):
    placed = (
        P("tiles", "nests", None),
        P("nests", "tiles", None, None),
        P(),
        P(),
        P(),
        P("nests", None),
    )
    return jax.shard_map(
        shards,
        mesh=mesh,
        in_specs=placed,
        out_specs=(P("tiles", "nests", None), P("nests", "tiles", None, None)),
        check_vma=False,
    )
```

```python
import functools

import jax
import jax.numpy as jnp
from jax import lax
from jax.experimental import pallas as pl
from jax.experimental.pallas import tpu as pltpu
from jax.sharding import PartitionSpec as P

STEPS = 3
KAPPA = 0.125
C = 48
WIDE = 56
SIDE = 4
GROUP_ROWS = 8
DEV_ROWS = 4
FB_SLOTS = 3
FB_GROUP = 7
FB_WINDOW = 22
F32 = jnp.float32
BF16 = jnp.bfloat16


def third(value):
    return lax.div(value, jnp.int32(3))


def wrap(value):
    return lax.rem(value + 2 * SIDE, jnp.int32(SIDE))


def split(value):
    high = value.astype(BF16)
    return high, (value - high.astype(F32)).astype(BF16)


def wide_weights(matrix):
    high, low = split(matrix)
    row = jnp.concatenate([high, low], axis=1)
    return jnp.concatenate([row, row], axis=0)


def mix(value, weights):
    lhs = jnp.concatenate(split(value), axis=1)
    both = jnp.dot(lhs, weights, preferred_element_type=F32)
    half = both.shape[1] // 2
    return both[:, :half] + both[:, half:]


def choose(way, values):
    result = values[-1]
    for k in range(len(values) - 2, -1, -1):
        result = jnp.where(way == k, values[k], result)
    return result


def eye(size):
    shape = (size, size)
    return lax.broadcasted_iota(jnp.int32, shape, 0) == lax.broadcasted_iota(jnp.int32, shape, 1)


def nest_weights(nest_mix, courant):
    c0, c1 = courant[0:1, :], courant[1:2, :]
    stay = jnp.where(eye(nest_mix.shape[0]), 1.0 - c0 - c1, 0.0)
    return c0, c1, wide_weights(nest_mix[...] + stay)


def owner_place(row, first, tile_rows):
    owner = lax.div(jnp.maximum(row, 0), jnp.int32(tile_rows))
    base = owner * tile_rows
    begin = jnp.clip(first - base, 0, tile_rows - GROUP_ROWS)
    return owner, jnp.clip(row - base - begin, 0, GROUP_ROWS - 1)


def pack_kernel(tile_rows, tile_cols, nest_rows, pos, parent, nest, b0, b1, b2, b3, west, east, down, up, band, cols, sems):
    tile = lax.axis_index("tiles")
    line = lax.axis_index("nests")
    my_y = lax.div(tile, jnp.int32(SIDE))
    corner = third(pos[0, 1]) - line * tile_cols
    aligned = pl.multiple_of(lax.div(corner, jnp.int32(8)) * 8, 8)
    shift = corner - aligned
    copies = []
    for k in range(SIDE):
        group = wrap(my_y + k)
        first = third(pos[0, 0] + SIDE * nest_rows * group) - 1
        begin = jnp.clip(first - tile * tile_rows, 0, tile_rows - GROUP_ROWS)
        copies.append(
            pltpu.make_async_copy(
                parent.at[pl.ds(begin, GROUP_ROWS), pl.ds(aligned, WIDE)], band.at[k], sems.at[k]
            )
        )
    halo = 3
    others = [
        pltpu.make_async_copy(parent.at[:, pl.ds(0, 8)], cols.at[0], sems.at[4]),
        pltpu.make_async_copy(parent.at[:, pl.ds(tile_cols - 8, 8)], cols.at[1], sems.at[5]),
        pltpu.make_async_copy(parent.at[tile_rows - 1], down.at[pl.ds(0, tile_cols)], sems.at[6]),
        pltpu.make_async_copy(parent.at[0], up, sems.at[7]),
    ]
    nest_cols = nest.shape[1]
    for r in range(halo):
        others.append(
            pltpu.make_async_copy(
                nest.at[nest_rows - halo + r],
                down.at[pl.ds(tile_cols + r * nest_cols, nest_cols)],
                sems.at[8 + r],
            )
        )
    for copy in copies + others:
        copy.start()
    for k, out in enumerate((b0, b1, b2, b3)):
        copies[k].wait()
        for r in range(GROUP_ROWS):
            out[r] = band[k, r, pl.ds(shift, C), :]
    others[0].wait()
    west[...] = cols[0, :, 0, :]
    others[1].wait()
    east[...] = cols[1, :, 7, :]
    for copy in others[2:]:
        copy.wait()


def pick_kernel(tile_rows, nest_rows, pos, fed, west, east, r0, r1, r2, r3, o0, o1, o2, o3, west_out, east_out):
    tile = lax.axis_index("tiles")
    my_y, my_z = lax.div(tile, jnp.int32(SIDE)), lax.rem(tile, jnp.int32(SIDE))
    first = third(pos[0, 0] + SIDE * nest_rows * my_y) - 1
    west_out[...] = west[...]
    east_out[...] = east[...]
    for k, out in enumerate((o0, o1, o2, o3)):
        target = my_y * SIDE + wrap(my_z + k)
        top = third(pos[0, 0] + nest_rows * target) - 1
        for j in range(DEV_ROWS):
            owner, place = owner_place(top + j, first, tile_rows)
            way = wrap(my_y - lax.div(owner, jnp.int32(SIDE)))
            out[j] = choose(way, [ref[place] for ref in (r0, r1, r2, r3)])
        for s in range(FB_SLOTS):
            out[DEV_ROWS + s] = fed[s]


def nest_kernel(tile_rows, tile_cols, pos, r0, r1, r2, r3, state, down, nest_mix, courant, out, lines, start, cur):
    tile = lax.axis_index("tiles")
    my_y, my_z = lax.div(tile, jnp.int32(SIDE)), lax.rem(tile, jnp.int32(SIDE))
    nest_rows, ncols, width = state.shape
    halo = STEPS
    ox, oy = pos[0, 0], pos[0, 1]
    phase = lax.rem(oy, jnp.int32(3))
    top = third(ox + nest_rows * tile) - 1
    spot = lax.broadcasted_iota(jnp.int32, (ncols, C), 0) + phase
    near = third(spot)
    frac = spot - 3 * near
    place = lax.broadcasted_iota(jnp.int32, (ncols, C), 1)
    table = jnp.where(place == near, 3 - frac, jnp.where(place == near + 1, frac, 0))
    table = table.astype(F32).astype(BF16)
    for j in range(DEV_ROWS):
        owner = lax.div(jnp.maximum(top + j, 0), jnp.int32(tile_rows))
        way = wrap(my_z - lax.rem(owner, jnp.int32(SIDE)))
        high, low = split(choose(way, [ref[j] for ref in (r0, r1, r2, r3)]))
        lines[j] = jnp.dot(table, high, preferred_element_type=F32) + jnp.dot(
            table, low, preferred_element_type=F32
        )
    for x in range(-halo, nest_rows):
        at = ox + nest_rows * tile + x
        at = jnp.maximum(at, 0)
        near_row = jnp.clip(third(at) - top, 0, DEV_ROWS - 2)
        part = lax.rem(at, jnp.int32(3)).astype(F32)
        interp = (3.0 - part) * lines[near_row] + part * lines[near_row + 1]
        own = state[x] if x >= 0 else down[pl.ds(tile_cols + (x + halo) * ncols, ncols), :]
        start[x + halo] = 0.5 * (own + interp * (1.0 / 9.0))
    first = tile == 0

    @pl.when(first)
    def _():
        for x in range(halo):
            start[x] = start[halo]

    c0, c1, weights = nest_weights(nest_mix, courant)
    edge_row = lax.broadcasted_iota(jnp.int32, (ncols, width), 0) == 0
    source = start
    for step in range(STEPS):
        last = step == STEPS - 1
        for r in range(nest_rows + halo - 1, step, -1):
            value = source[r]
            left = jnp.where(edge_row, start[r, 0:1, :], pltpu.roll(value, 1, 0))
            value = mix(value, weights) + c0 * source[r - 1] + c1 * left
            if r < halo:
                value = jnp.where(first, start[halo], value)
            if last:
                out[r - halo] = value
            else:
                cur[step, r] = value
        source = cur.at[step]


def up_third(value):
    return third(value + 2)


def feed_kernel(pos, state, nest_mix, courant, fb, start, cur):
    tile = lax.axis_index("tiles")
    nest_rows, ncols, width = state.shape
    rows = nest_rows + STEPS
    ox, oy = pos[0, 0], pos[0, 1]
    for x in range(rows):
        start[x] = 0.5 * state[x] if x < nest_rows else jnp.zeros((ncols, width), F32)
    above = jnp.where(tile == 0, start[0], 0.0)
    c0, c1, weights = nest_weights(nest_mix, courant)
    edge_row = lax.broadcasted_iota(jnp.int32, (ncols, width), 0) == 0

    def advanced(value, upper, edge):
        left = jnp.where(edge_row, edge, pltpu.roll(value, 1, 0))
        return mix(value, weights) + c0 * upper + c1 * left

    source = start
    for step in range(STEPS - 1):
        for r in range(nest_rows + step + 1):
            upper = above if r == 0 else source[r - 1]
            cur[step, r] = advanced(source[r], upper, start[r, 0:1, :])
        for r in range(nest_rows + step + 1, rows):
            cur[step, r] = jnp.zeros((ncols, width), F32)
        source = cur.at[step]
    rem_y = lax.rem(3 - lax.rem(oy, jnp.int32(3)), jnp.int32(3))
    slot = lax.broadcasted_iota(jnp.int32, (C, ncols), 0)
    pick = (lax.broadcasted_iota(jnp.int32, (C, ncols), 1) == rem_y + 3 * slot).astype(F32).astype(BF16)
    pick = jnp.concatenate([pick, pick], axis=1)
    first = up_third(ox + nest_rows * tile) * 3 - ox - nest_rows * tile
    for s in range(FB_SLOTS):
        r = jnp.minimum(first + 3 * s, rows - 1)
        upper = source[jnp.maximum(r - 1, 0)]
        if s == 0:
            upper = jnp.where(r == 0, above, upper)
        value = advanced(source[r], upper, start[r, 0:1, :])
        fb[s] = jnp.dot(pick, jnp.concatenate(split(value), axis=0), preferred_element_type=F32)


def combine_kernel(nest_rows, pos, e0, e1, e2, e3, out):
    tile = lax.axis_index("tiles")
    my_y, my_z = lax.div(tile, jnp.int32(SIDE)), lax.rem(tile, jnp.int32(SIDE))
    ox = pos[0, 0]
    base = up_third(ox + SIDE * nest_rows * my_y)
    for r in range(FB_GROUP):
        out[r] = jnp.zeros(out.shape[1:], F32)
    for k, ref in enumerate((e0, e1, e2, e3)):
        origin = ox + nest_rows * (SIDE * my_y + wrap(my_z - k))
        row = up_third(origin)
        for s in range(FB_SLOTS):

            @pl.when(3 * (row + s) - origin < nest_rows + STEPS)
            def _(ref=ref, row=row, s=s):
                out[row + s - base] += ref[DEV_ROWS + s]


def window(pos, tile_rows, tile_cols, total):
    ox, oy = pos[0, 0], pos[0, 1]
    first_row = lax.axis_index("tiles") * tile_rows
    low_row, high_row = up_third(ox), third(ox + total - 1)
    owns = (high_row >= first_row) & (low_row < first_row + tile_rows)
    begin = jnp.clip(low_row - first_row, 0, tile_rows - FB_WINDOW)
    corner = third(oy) - lax.axis_index("nests") * tile_cols
    aligned = pl.multiple_of(lax.div(corner, jnp.int32(8)) * 8, 8)
    shift = corner - aligned + up_third(oy) - third(oy)
    return owns, first_row, begin, aligned, shift, up_third(oy) * 3 - oy


def own_kernel(tile_rows, tile_cols, total, pos, parent, from_up, nest_mix, courant, out, buf, parts, sems):
    owns, first_row, begin, aligned, shift, rem_y = window(pos, tile_rows, tile_cols, total)
    ox = pos[0, 0]
    width = buf.shape[2]

    @pl.when(owns)
    def _():
        cols = pl.ds(aligned, WIDE)
        main = pltpu.make_async_copy(
            parent.at[pl.ds(begin, FB_WINDOW), cols], buf.at[pl.ds(1, FB_WINDOW), pl.ds(8, WIDE)], sems.at[0]
        )
        edge = pltpu.make_async_copy(
            parent.at[jnp.maximum(begin - 1, 0), cols], buf.at[0, pl.ds(8, WIDE)], sems.at[1]
        )
        main.start()
        edge.start()
        buf[:, 0:8, :] = jnp.zeros((FB_WINDOW + 1, 8, width), F32)

        c0, c1 = courant[0:1, :], courant[1:2, :]
        diagonal = eye(width)
        r0 = jnp.sum(jnp.where(diagonal, c0, 0.0), axis=1, keepdims=True)
        r1 = jnp.sum(jnp.where(diagonal, c1, 0.0), axis=1, keepdims=True)
        one = nest_mix[...] + jnp.where(diagonal, 1.0 - c0 - c1, 0.0)
        weights = wide_weights(one)
        many = mix(jnp.concatenate([one, one * c0, one * c1], axis=0), weights)
        two, by0, by1 = many[:width], many[width : 2 * width], many[2 * width :]
        paths = {
            (0, 0): mix(two, weights),
            (1, 0): r0 * two + by0 + two * c0,
            (0, 1): r1 * two + by1 + two * c1,
            (2, 0): (r0 * r0) * one + (r0 * one) * c0 + one * (c0 * c0),
            (0, 2): (r1 * r1) * one + (r1 * one) * c1 + one * (c1 * c1),
            (1, 1): (2.0 * r0 * r1) * one + (r0 * one) * c1 + (r1 * one) * c0 + one * (2.0 * c0 * c1),
            (3, 0): jnp.where(diagonal, c0 * c0 * c0, 0.0),
            (0, 3): jnp.where(diagonal, c1 * c1 * c1, 0.0),
            (2, 1): jnp.where(diagonal, 3.0 * c0 * c0 * c1, 0.0),
            (1, 2): jnp.where(diagonal, 3.0 * c0 * c1 * c1, 0.0),
        }

        def corner(low_row, low_col):
            sum_of = jnp.zeros((width, width), F32)
            for (i, j), path in paths.items():
                weight = (i if low_row else 3 - i) * (j if low_col else 3 - j) * (0.5 / 9.0)
                if weight:
                    sum_of = sum_of + weight * path
            return wide_weights(sum_of)

        this_row = jnp.concatenate([corner(False, False), corner(False, True)], axis=0)
        row_before = jnp.concatenate([corner(True, False), corner(True, True)], axis=0)

        main.wait()
        edge.wait()

        @pl.when(begin == 0)
        def _():
            buf[0, pl.ds(8, WIDE), :] = from_up[pl.ds(aligned, WIDE), :]

        for w in range(FB_WINDOW + 1):
            near = buf[w, pl.ds(8 + shift, C), :]
            back = buf[w, pl.ds(7 + shift, C), :]
            parts[w] = jnp.concatenate(split(near) + split(back), axis=1)
        batch = FB_WINDOW // 2
        for w in range(0, FB_WINDOW, batch):
            this = parts[w + 1 : w + 1 + batch].reshape(batch * C, 4 * width)
            before = parts[w : w + batch].reshape(batch * C, 4 * width)
            both = jnp.dot(this, this_row, preferred_element_type=F32) + jnp.dot(
                before, row_before, preferred_element_type=F32
            )
            out[w : w + batch] = (both[:, :width] + both[:, width:]).reshape(batch, C, width)

        first = up_third(ox) - first_row - begin
        at = jnp.clip(first, 0, FB_WINDOW - 1)
        pad = jnp.zeros((24 - FB_WINDOW, width), F32)

        def gather(k, offset):
            column = buf[pl.ds(k, FB_WINDOW), pl.ds(offset + shift, 1), :].reshape(FB_WINDOW, width)
            return jnp.concatenate([buf[at + k, pl.ds(offset + shift, C), :], column, pad], axis=0)

        near = [gather(k, 8) for k in range(2)]
        back = [gather(k, 7) for k in range(2)]
        line = lax.broadcasted_iota(jnp.int32, near[0].shape, 0)
        in_row = line < C
        x = 3 * (first_row + begin + jnp.where(in_row, at, line - C)) - ox
        y = rem_y + 3 * jnp.where(in_row, line, 0)
        start = {}
        for i in range(STEPS + 1):
            lean = jnp.minimum(x, i).astype(F32) * (0.5 / 9.0)
            rest = 0.5 / 3.0 - lean
            right = rest * near[1] + lean * near[0]
            left = rest * back[1] + lean * back[0]
            for j in range(STEPS + 1 - i):
                tilt = jnp.minimum(y, j).astype(F32)
                start[i, j] = right * (3.0 - tilt) + left * tilt
        cells = start
        size = C + 24
        for step in range(STEPS):
            keys = [(i, j) for i in range(STEPS - step) for j in range(STEPS - step - i)]
            mixed = mix(jnp.concatenate([cells[key] for key in keys], axis=0), weights)
            fresh = {}
            for n, (i, j) in enumerate(keys):
                value = mixed[n * size : (n + 1) * size] + c0 * cells[i + 1, j] + c1 * cells[i, j + 1]
                fresh[i, j] = jnp.where((x < i) | (y < j), start[i, j], value)
            cells = fresh
        edges = cells[0, 0]

        @pl.when((first >= 0) & (first < FB_WINDOW))
        def _():
            out[at] = edges[:C]

        for w in range(FB_WINDOW):
            out[w, 0:1, :] = edges[C + w : C + w + 1]


def patch_kernel(tile_rows, tile_cols, nest_rows, ncols, pos, parent, own, g0, g1, g2, g3, out, buf, sems):
    total = nest_rows * SIDE * SIDE
    owns, first_row, begin, aligned, shift, rem_y = window(pos, tile_rows, tile_cols, total)
    my_y = lax.div(lax.axis_index("tiles"), jnp.int32(SIDE))
    ox = pos[0, 0]
    span = SIDE * nest_rows

    @pl.when(owns)
    def _():
        place = (pl.ds(begin, FB_WINDOW), pl.ds(aligned, WIDE))
        copy = pltpu.make_async_copy(parent.at[place], buf, sems.at[0])
        copy.start()
        copy.wait()
        live = rem_y + 3 * lax.broadcasted_iota(jnp.int32, (C, buf.shape[2]), 0) < ncols

        @pl.loop(0, FB_WINDOW)
        def _(w):
            row = first_row + begin + w
            x = 3 * row - ox

            @pl.when((x >= 0) & (x < total))
            def _():
                def from_group(group):
                    r = jnp.clip(row - up_third(ox + span * group), 0, FB_GROUP - 1)
                    return choose(wrap(my_y - group), [ref[r] for ref in (g0, g1, g2, g3)])

                group = lax.div(x, jnp.int32(span))
                value = own[w] + from_group(group)
                spilt = (group > 0) & (x - span * group < STEPS)
                value = value + jnp.where(spilt, from_group(jnp.maximum(group - 1, 0)), 0.0)
                old = buf[w, pl.ds(shift, C), :]
                buf[w, pl.ds(shift, C), :] = jnp.where(live, 0.5 * (old + value), old)

        back = pltpu.make_async_copy(buf, out.at[place], sems.at[1])
        back.start()
        back.wait()


def parent_kernel(rows, parent, from_up, from_down, west, east, parent_mix, out, token, full, done, weights, in_sems, out_sems):
    height, cols = parent.shape[0], parent.shape[1]
    count = height // rows

    def fetch(i):
        return pltpu.make_async_copy(
            parent.at[pl.ds(i * rows, rows)], full.at[pl.ds(1 + i * rows, rows)], in_sems.at[i]
        )

    def store(i):
        slot = lax.rem(i, 2)
        return pltpu.make_async_copy(done.at[slot], out.at[pl.ds(i * rows, rows)], out_sems.at[slot])

    for i in range(count):
        fetch(i).start()
    size = parent_mix.shape[0]
    weights[...] = wide_weights(parent_mix[...] + jnp.where(eye(size), 1.0 - 4.0 * KAPPA, 0.0))
    full[0] = from_up[pl.ds(0, cols), :]
    full[height + 1] = from_down[...]
    index = lax.broadcasted_iota(jnp.int32, (cols, size), 0)
    low_edge, high_edge = index == 0, index == cols - 1
    fetch(0).wait()

    @pl.loop(0, count)
    def _(i):
        @pl.when(i + 1 < count)
        def _():
            fetch(i + 1).wait()

        @pl.when(i >= 2)
        def _():
            store(i - 2).wait()

        slot = lax.rem(i, 2)
        for r in range(rows):
            at = i * rows + r
            value = full[at + 1]
            left = jnp.where(low_edge, west[pl.ds(at, 1), :], pltpu.roll(value, 1, 0))
            right = jnp.where(high_edge, east[pl.ds(at, 1), :], pltpu.roll(value, cols - 1, 0))
            beside = (full[at] + full[at + 2]) + (left + right)
            done[slot, r] = mix(value, weights[...]) + KAPPA * beside
        store(i).start()

    store(count - 2).wait()
    store(count - 1).wait()
    token[...] = jnp.zeros(token.shape, F32)


def smem():
    return pl.BlockSpec(memory_space=pltpu.SMEM)


def vmem():
    return pl.BlockSpec(memory_space=pltpu.VMEM)


def hbm():
    return pl.BlockSpec(memory_space=pltpu.HBM)


def run(name, kernel, ins, outs, scratch=(), after=(), room=50, flops=0, moved=1, **options):
    given, held = len(ins), len(after)

    def body(*refs):
        kernel(*refs[:given], *refs[given + held :])

    return pl.pallas_call(
        body,
        out_shape=[shape for _, shape in outs],
        in_specs=[spec for spec, _ in ins] + [pl.BlockSpec(memory_space=pl.ANY)] * held,
        out_specs=[spec for spec, _ in outs],
        scratch_shapes=list(scratch),
        compiler_params=pltpu.CompilerParams(vmem_limit_bytes=room << 20),
        cost_estimate=pl.CostEstimate(flops=flops, bytes_accessed=moved << 20, transcendentals=0),
        name=name,
        **options,
    )(*[value for _, value in ins], *after)


def y_route(k):
    return [(t, (t + SIDE * k) % (SIDE * SIDE)) for t in range(SIDE * SIDE)]


def z_route(k):
    return [(t, t // SIDE * SIDE + (t + k) % SIDE) for t in range(SIDE * SIDE)]


def shards(parent, nest_state, parent_mix, nest_mix, courant, nest_pos):
    tile_rows, tile_cols, width = parent.shape
    state = nest_state[0]
    nest_rows, ncols, _ = state.shape
    total = nest_rows * SIDE * SIDE
    count = SIDE * SIDE
    lines = lax.axis_size("nests")
    S, V, H = smem(), vmem(), hbm()
    big = 50

    def f(*shape):
        return jax.ShapeDtypeStruct(shape, F32)

    def on_tiles(block, route):
        return lax.ppermute(block, "tiles", route)

    packed = run(
        "pack",
        functools.partial(pack_kernel, tile_rows, tile_cols, nest_rows),
        [(S, nest_pos), (H, parent), (H, state)],
        [(V, f(GROUP_ROWS, C, width))] * SIDE
        + [(V, f(tile_rows, width))] * 2
        + [(V, f(tile_cols + STEPS * ncols, width)), (V, f(tile_cols, width))],
        [
            pltpu.VMEM((SIDE, GROUP_ROWS, WIDE, width), F32),
            pltpu.VMEM((2, tile_rows, 8, width), F32),
            pltpu.SemaphoreType.DMA((11,)),
        ],
        moved=4,
    )
    b, (west_out, east_out, down_out, up_out) = packed[:4], packed[4:]
    got = {k: on_tiles(b[k], y_route(k)) for k in (1, 3, 2)}
    from_up = on_tiles(down_out, [(i, i + 1) for i in range(count - 1)])
    from_down = on_tiles(up_out, [(i + 1, i) for i in range(count - 1)])

    (fed,) = run(
        "feed",
        feed_kernel,
        [(S, nest_pos), (V, state), (V, nest_mix), (V, courant)],
        [(V, f(FB_SLOTS, C, width))],
        [
            pltpu.VMEM((nest_rows + STEPS, ncols, width), F32),
            pltpu.VMEM((STEPS - 1, nest_rows + STEPS, ncols, width), F32),
        ],
        after=[west_out],
        flops=1 << 28,
        moved=4,
    )
    picked = run(
        "pick",
        functools.partial(pick_kernel, tile_rows, nest_rows),
        [(S, nest_pos)] + [(V, x) for x in (fed, west_out, east_out, b[0], got[1], got[2], got[3])],
        [(V, f(DEV_ROWS + FB_SLOTS, C, width))] * SIDE + [(V, f(tile_rows, width))] * 2,
    )
    mine = {k: on_tiles(picked[k], z_route(k)) for k in (1, 3, 2)}
    west = lax.ppermute(picked[5], "nests", [(i, i + 1) for i in range(lines - 1)])
    east = lax.ppermute(picked[4], "nests", [(i + 1, i) for i in range(lines - 1)])
    (own,) = run(
        "own_feed",
        functools.partial(own_kernel, tile_rows, tile_cols, total),
        [(S, nest_pos), (H, parent), (V, from_up), (V, nest_mix), (V, courant)],
        [(V, f(FB_WINDOW, C, width))],
        [
            pltpu.VMEM((FB_WINDOW + 1, WIDE + 8, width), F32),
            pltpu.VMEM((FB_WINDOW + 1, C, 4 * width), BF16),
            pltpu.SemaphoreType.DMA((2,)),
        ],
        after=[picked[0]],
        flops=1 << 30,
        moved=8,
    )
    (joined,) = run(
        "combine",
        functools.partial(combine_kernel, nest_rows),
        [(S, nest_pos), (V, picked[0])] + [(V, mine[k]) for k in (1, 2, 3)],
        [(V, f(FB_GROUP, C, width))],
        after=[own],
    )
    groups = {k: on_tiles(joined, y_route(k)) for k in (1, 3, 2)}

    rows = 8
    parent_new, token = run(
        "parent_step",
        functools.partial(parent_kernel, rows),
        [(H, parent)] + [(V, x) for x in (from_up, from_down, west, east, parent_mix)],
        [(H, f(tile_rows, tile_cols, width)), (V, f(8, width))],
        [
            pltpu.VMEM((tile_rows + 2, tile_cols, width), F32),
            pltpu.VMEM((2, rows, tile_cols, width), F32),
            pltpu.VMEM((2 * width, 2 * width), BF16),
            pltpu.SemaphoreType.DMA((tile_rows // rows,)),
            pltpu.SemaphoreType.DMA((2,)),
        ],
        after=[joined],
        room=big,
        flops=2 * tile_rows * tile_cols * 256 * 256,
        moved=20,
    )
    (nest_out,) = run(
        "nest_steps",
        functools.partial(nest_kernel, tile_rows, tile_cols),
        [(S, nest_pos), (V, picked[0])]
        + [(V, mine[k]) for k in (1, 2, 3)]
        + [(V, x) for x in (state, from_up, nest_mix, courant)],
        [(V, f(nest_rows, ncols, width))],
        [
            pltpu.VMEM((DEV_ROWS, ncols, width), F32),
            pltpu.VMEM((nest_rows + STEPS, ncols, width), F32),
            pltpu.VMEM((STEPS - 1, nest_rows + STEPS, ncols, width), F32),
        ],
        after=[token],
        flops=1 << 28,
        moved=6,
    )
    (parent_out,) = run(
        "patch",
        functools.partial(patch_kernel, tile_rows, tile_cols, nest_rows, ncols),
        [(S, nest_pos), (H, parent_new), (V, own), (V, joined)] + [(V, groups[k]) for k in (1, 2, 3)],
        [(H, f(tile_rows, tile_cols, width))],
        [pltpu.VMEM((FB_WINDOW, WIDE, width), F32), pltpu.SemaphoreType.DMA((2,))],
        room=big,
        moved=2,
        input_output_aliases={1: 0},
    )
    return parent_out, nest_out[None]


def solution(mesh):
    placed = (
        P("tiles", "nests", None),
        P("nests", "tiles", None, None),
        P(),
        P(),
        P(),
        P("nests", None),
    )
    return jax.shard_map(
        shards,
        mesh=mesh,
        in_specs=placed,
        out_specs=(P("tiles", "nests", None), P("nests", "tiles", None, None)),
        check_vma=False,
    )
```

```python
import functools

import jax
import jax.numpy as jnp
from jax import lax
from jax.experimental import pallas as pl
from jax.experimental.pallas import tpu as pltpu
from jax.sharding import PartitionSpec as P

STEPS = 3
KAPPA = 0.125
C = 48
WIDE = 56
SIDE = 4
GROUP_ROWS = 8
DEV_ROWS = 4
FB_SLOTS = 3
FB_GROUP = 7
FB_WINDOW = 22
F32 = jnp.float32
BF16 = jnp.bfloat16


def third(value):
    return lax.div(value, jnp.int32(3))


def wrap(value):
    return lax.rem(value + 2 * SIDE, jnp.int32(SIDE))


def split(value):
    high = value.astype(BF16)
    return high, (value - high.astype(F32)).astype(BF16)


def wide_weights(matrix):
    high, low = split(matrix)
    row = jnp.concatenate([high, low], axis=1)
    return jnp.concatenate([row, row], axis=0)


def mix(value, weights):
    lhs = jnp.concatenate(split(value), axis=1)
    both = jnp.dot(lhs, weights, preferred_element_type=F32)
    half = both.shape[1] // 2
    return both[:, :half] + both[:, half:]


def choose(way, values):
    result = values[-1]
    for k in range(len(values) - 2, -1, -1):
        result = jnp.where(way == k, values[k], result)
    return result


def eye(size):
    shape = (size, size)
    return lax.broadcasted_iota(jnp.int32, shape, 0) == lax.broadcasted_iota(jnp.int32, shape, 1)


def nest_weights(nest_mix, courant):
    c0, c1 = courant[0:1, :], courant[1:2, :]
    stay = jnp.where(eye(nest_mix.shape[0]), 1.0 - c0 - c1, 0.0)
    return c0, c1, wide_weights(nest_mix[...] + stay)


def owner_place(row, first, tile_rows):
    owner = lax.div(jnp.maximum(row, 0), jnp.int32(tile_rows))
    base = owner * tile_rows
    begin = jnp.clip(first - base, 0, tile_rows - GROUP_ROWS)
    return owner, jnp.clip(row - base - begin, 0, GROUP_ROWS - 1)


def pack_kernel(tile_rows, tile_cols, nest_rows, pos, parent, b0, b1, b2, b3, west, east, down, up, band, cols, sems):
    tile = lax.axis_index("tiles")
    line = lax.axis_index("nests")
    my_y = lax.div(tile, jnp.int32(SIDE))
    corner = third(pos[0, 1]) - line * tile_cols
    aligned = pl.multiple_of(lax.div(corner, jnp.int32(8)) * 8, 8)
    shift = corner - aligned
    copies = []
    for k in range(SIDE):
        group = wrap(my_y + k)
        first = third(pos[0, 0] + SIDE * nest_rows * group) - 1
        begin = jnp.clip(first - tile * tile_rows, 0, tile_rows - GROUP_ROWS)
        copies.append(
            pltpu.make_async_copy(
                parent.at[pl.ds(begin, GROUP_ROWS), pl.ds(aligned, WIDE)], band.at[k], sems.at[k]
            )
        )
    others = [
        pltpu.make_async_copy(parent.at[:, pl.ds(0, 8)], cols.at[0], sems.at[4]),
        pltpu.make_async_copy(parent.at[:, pl.ds(tile_cols - 8, 8)], cols.at[1], sems.at[5]),
        pltpu.make_async_copy(parent.at[tile_rows - 1], down, sems.at[6]),
        pltpu.make_async_copy(parent.at[0], up, sems.at[7]),
    ]
    for copy in copies + others:
        copy.start()
    for k, out in enumerate((b0, b1, b2, b3)):
        copies[k].wait()
        for r in range(GROUP_ROWS):
            out[r] = band[k, r, pl.ds(shift, C), :]
    others[0].wait()
    west[...] = cols[0, :, 0, :]
    others[1].wait()
    east[...] = cols[1, :, 7, :]
    for copy in others[2:]:
        copy.wait()


def pick_kernel(tile_rows, nest_rows, pos, fed, west, east, r0, r1, r2, r3, o0, o1, o2, o3, west_out, east_out):
    tile = lax.axis_index("tiles")
    my_y, my_z = lax.div(tile, jnp.int32(SIDE)), lax.rem(tile, jnp.int32(SIDE))
    first = third(pos[0, 0] + SIDE * nest_rows * my_y) - 1
    west_out[...] = west[...]
    east_out[...] = east[...]
    for k, out in enumerate((o0, o1, o2, o3)):
        target = my_y * SIDE + wrap(my_z + k)
        top = third(pos[0, 0] + nest_rows * target) - 1
        for j in range(DEV_ROWS):
            owner, place = owner_place(top + j, first, tile_rows)
            way = wrap(my_y - lax.div(owner, jnp.int32(SIDE)))
            out[j] = choose(way, [ref[place] for ref in (r0, r1, r2, r3)])
        for s in range(FB_SLOTS):
            out[DEV_ROWS + s] = fed[s]


def nest_kernel(tile_rows, tile_cols, pos, r0, r1, r2, r3, state, tail, nest_mix, courant, out, lines, start, cur):
    tile = lax.axis_index("tiles")
    my_y, my_z = lax.div(tile, jnp.int32(SIDE)), lax.rem(tile, jnp.int32(SIDE))
    nest_rows, ncols, width = state.shape
    halo = STEPS
    ox, oy = pos[0, 0], pos[0, 1]
    phase = lax.rem(oy, jnp.int32(3))
    top = third(ox + nest_rows * tile) - 1
    spot = lax.broadcasted_iota(jnp.int32, (ncols, C), 0) + phase
    near = third(spot)
    frac = spot - 3 * near
    place = lax.broadcasted_iota(jnp.int32, (ncols, C), 1)
    table = jnp.where(place == near, 3 - frac, jnp.where(place == near + 1, frac, 0))
    table = table.astype(F32).astype(BF16)
    for j in range(DEV_ROWS):
        owner = lax.div(jnp.maximum(top + j, 0), jnp.int32(tile_rows))
        way = wrap(my_z - lax.rem(owner, jnp.int32(SIDE)))
        high, low = split(choose(way, [ref[j] for ref in (r0, r1, r2, r3)]))
        lines[j] = jnp.dot(table, high, preferred_element_type=F32) + jnp.dot(
            table, low, preferred_element_type=F32
        )
    for x in range(-halo, nest_rows):
        at = ox + nest_rows * tile + x
        at = jnp.maximum(at, 0)
        near_row = jnp.clip(third(at) - top, 0, DEV_ROWS - 2)
        part = lax.rem(at, jnp.int32(3)).astype(F32)
        interp = (3.0 - part) * lines[near_row] + part * lines[near_row + 1]
        own = state[x] if x >= 0 else tail[x + halo]
        start[x + halo] = 0.5 * (own + interp * (1.0 / 9.0))
    first = tile == 0

    @pl.when(first)
    def _():
        for x in range(halo):
            start[x] = start[halo]

    c0, c1, weights = nest_weights(nest_mix, courant)
    edge_row = lax.broadcasted_iota(jnp.int32, (ncols, width), 0) == 0
    source = start
    for step in range(STEPS):
        last = step == STEPS - 1
        for r in range(nest_rows + halo - 1, step, -1):
            value = source[r]
            left = jnp.where(edge_row, start[r, 0:1, :], pltpu.roll(value, 1, 0))
            value = mix(value, weights) + c0 * source[r - 1] + c1 * left
            if r < halo:
                value = jnp.where(first, start[halo], value)
            if last:
                out[r - halo] = value
            else:
                cur[step, r] = value
        source = cur.at[step]


def up_third(value):
    return third(value + 2)


def feed_kernel(pos, state, nest_mix, courant, fb, tail, start, cur):
    tile = lax.axis_index("tiles")
    nest_rows, ncols, width = state.shape
    rows = nest_rows + STEPS
    ox, oy = pos[0, 0], pos[0, 1]
    tail[...] = state[nest_rows - STEPS :]
    for x in range(rows):
        start[x] = 0.5 * state[x] if x < nest_rows else jnp.zeros((ncols, width), F32)
    above = jnp.where(tile == 0, start[0], 0.0)
    c0, c1, weights = nest_weights(nest_mix, courant)
    edge_row = lax.broadcasted_iota(jnp.int32, (ncols, width), 0) == 0

    def advanced(value, upper, edge):
        left = jnp.where(edge_row, edge, pltpu.roll(value, 1, 0))
        return mix(value, weights) + c0 * upper + c1 * left

    source = start
    for step in range(STEPS - 1):
        for r in range(nest_rows + step + 1):
            upper = above if r == 0 else source[r - 1]
            cur[step, r] = advanced(source[r], upper, start[r, 0:1, :])
        for r in range(nest_rows + step + 1, rows):
            cur[step, r] = jnp.zeros((ncols, width), F32)
        source = cur.at[step]
    rem_y = lax.rem(3 - lax.rem(oy, jnp.int32(3)), jnp.int32(3))
    slot = lax.broadcasted_iota(jnp.int32, (C, ncols), 0)
    pick = (lax.broadcasted_iota(jnp.int32, (C, ncols), 1) == rem_y + 3 * slot).astype(F32).astype(BF16)
    pick = jnp.concatenate([pick, pick], axis=1)
    first = up_third(ox + nest_rows * tile) * 3 - ox - nest_rows * tile
    for s in range(FB_SLOTS):
        r = jnp.minimum(first + 3 * s, rows - 1)
        upper = source[jnp.maximum(r - 1, 0)]
        if s == 0:
            upper = jnp.where(r == 0, above, upper)
        value = advanced(source[r], upper, start[r, 0:1, :])
        fb[s] = jnp.dot(pick, jnp.concatenate(split(value), axis=0), preferred_element_type=F32)


def combine_kernel(nest_rows, pos, e0, e1, e2, e3, out):
    tile = lax.axis_index("tiles")
    my_y, my_z = lax.div(tile, jnp.int32(SIDE)), lax.rem(tile, jnp.int32(SIDE))
    ox = pos[0, 0]
    base = up_third(ox + SIDE * nest_rows * my_y)
    for r in range(FB_GROUP):
        out[r] = jnp.zeros(out.shape[1:], F32)
    for k, ref in enumerate((e0, e1, e2, e3)):
        origin = ox + nest_rows * (SIDE * my_y + wrap(my_z - k))
        row = up_third(origin)
        for s in range(FB_SLOTS):

            @pl.when(3 * (row + s) - origin < nest_rows + STEPS)
            def _(ref=ref, row=row, s=s):
                out[row + s - base] += ref[DEV_ROWS + s]


def window(pos, tile_rows, tile_cols, total):
    ox, oy = pos[0, 0], pos[0, 1]
    first_row = lax.axis_index("tiles") * tile_rows
    low_row, high_row = up_third(ox), third(ox + total - 1)
    owns = (high_row >= first_row) & (low_row < first_row + tile_rows)
    begin = jnp.clip(low_row - first_row, 0, tile_rows - FB_WINDOW)
    corner = third(oy) - lax.axis_index("nests") * tile_cols
    aligned = pl.multiple_of(lax.div(corner, jnp.int32(8)) * 8, 8)
    shift = corner - aligned + up_third(oy) - third(oy)
    return owns, first_row, begin, aligned, shift, up_third(oy) * 3 - oy


def own_kernel(tile_rows, tile_cols, total, pos, parent, from_up, nest_mix, courant, out, buf, parts, sems):
    owns, first_row, begin, aligned, shift, rem_y = window(pos, tile_rows, tile_cols, total)
    ox = pos[0, 0]
    width = buf.shape[2]

    @pl.when(owns)
    def _():
        cols = pl.ds(aligned, WIDE)
        main = pltpu.make_async_copy(
            parent.at[pl.ds(begin, FB_WINDOW), cols], buf.at[pl.ds(1, FB_WINDOW), pl.ds(8, WIDE)], sems.at[0]
        )
        edge = pltpu.make_async_copy(
            parent.at[jnp.maximum(begin - 1, 0), cols], buf.at[0, pl.ds(8, WIDE)], sems.at[1]
        )
        main.start()
        edge.start()
        buf[:, 0:8, :] = jnp.zeros((FB_WINDOW + 1, 8, width), F32)

        c0, c1 = courant[0:1, :], courant[1:2, :]
        diagonal = eye(width)
        r0 = jnp.sum(jnp.where(diagonal, c0, 0.0), axis=1, keepdims=True)
        r1 = jnp.sum(jnp.where(diagonal, c1, 0.0), axis=1, keepdims=True)
        one = nest_mix[...] + jnp.where(diagonal, 1.0 - c0 - c1, 0.0)
        weights = wide_weights(one)
        many = mix(jnp.concatenate([one, one * c0, one * c1], axis=0), weights)
        two, by0, by1 = many[:width], many[width : 2 * width], many[2 * width :]
        paths = {
            (0, 0): mix(two, weights),
            (1, 0): r0 * two + by0 + two * c0,
            (0, 1): r1 * two + by1 + two * c1,
            (2, 0): (r0 * r0) * one + (r0 * one) * c0 + one * (c0 * c0),
            (0, 2): (r1 * r1) * one + (r1 * one) * c1 + one * (c1 * c1),
            (1, 1): (2.0 * r0 * r1) * one + (r0 * one) * c1 + (r1 * one) * c0 + one * (2.0 * c0 * c1),
            (3, 0): jnp.where(diagonal, c0 * c0 * c0, 0.0),
            (0, 3): jnp.where(diagonal, c1 * c1 * c1, 0.0),
            (2, 1): jnp.where(diagonal, 3.0 * c0 * c0 * c1, 0.0),
            (1, 2): jnp.where(diagonal, 3.0 * c0 * c1 * c1, 0.0),
        }

        def corner(low_row, low_col):
            sum_of = jnp.zeros((width, width), F32)
            for (i, j), path in paths.items():
                weight = (i if low_row else 3 - i) * (j if low_col else 3 - j) * (0.5 / 9.0)
                if weight:
                    sum_of = sum_of + weight * path
            return wide_weights(sum_of)

        this_row = jnp.concatenate([corner(False, False), corner(False, True)], axis=0)
        row_before = jnp.concatenate([corner(True, False), corner(True, True)], axis=0)

        main.wait()
        edge.wait()

        @pl.when(begin == 0)
        def _():
            buf[0, pl.ds(8, WIDE), :] = from_up[pl.ds(aligned, WIDE), :]

        for w in range(FB_WINDOW + 1):
            near = buf[w, pl.ds(8 + shift, C), :]
            back = buf[w, pl.ds(7 + shift, C), :]
            parts[w] = jnp.concatenate(split(near) + split(back), axis=1)
        batch = FB_WINDOW // 2
        for w in range(0, FB_WINDOW, batch):
            this = parts[w + 1 : w + 1 + batch].reshape(batch * C, 4 * width)
            before = parts[w : w + batch].reshape(batch * C, 4 * width)
            both = jnp.dot(this, this_row, preferred_element_type=F32) + jnp.dot(
                before, row_before, preferred_element_type=F32
            )
            out[w : w + batch] = (both[:, :width] + both[:, width:]).reshape(batch, C, width)

        first = up_third(ox) - first_row - begin
        at = jnp.clip(first, 0, FB_WINDOW - 1)
        pad = jnp.zeros((24 - FB_WINDOW, width), F32)

        def gather(k, offset):
            column = buf[pl.ds(k, FB_WINDOW), pl.ds(offset + shift, 1), :].reshape(FB_WINDOW, width)
            return jnp.concatenate([buf[at + k, pl.ds(offset + shift, C), :], column, pad], axis=0)

        near = [gather(k, 8) for k in range(2)]
        back = [gather(k, 7) for k in range(2)]
        line = lax.broadcasted_iota(jnp.int32, near[0].shape, 0)
        in_row = line < C
        x = 3 * (first_row + begin + jnp.where(in_row, at, line - C)) - ox
        y = rem_y + 3 * jnp.where(in_row, line, 0)
        start = {}
        for i in range(STEPS + 1):
            lean = jnp.minimum(x, i).astype(F32) * (0.5 / 9.0)
            rest = 0.5 / 3.0 - lean
            right = rest * near[1] + lean * near[0]
            left = rest * back[1] + lean * back[0]
            for j in range(STEPS + 1 - i):
                tilt = jnp.minimum(y, j).astype(F32)
                start[i, j] = right * (3.0 - tilt) + left * tilt
        cells = start
        size = C + 24
        for step in range(STEPS):
            keys = [(i, j) for i in range(STEPS - step) for j in range(STEPS - step - i)]
            mixed = mix(jnp.concatenate([cells[key] for key in keys], axis=0), weights)
            fresh = {}
            for n, (i, j) in enumerate(keys):
                value = mixed[n * size : (n + 1) * size] + c0 * cells[i + 1, j] + c1 * cells[i, j + 1]
                fresh[i, j] = jnp.where((x < i) | (y < j), start[i, j], value)
            cells = fresh
        edges = cells[0, 0]

        @pl.when((first >= 0) & (first < FB_WINDOW))
        def _():
            out[at] = edges[:C]

        for w in range(FB_WINDOW):
            out[w, 0:1, :] = edges[C + w : C + w + 1]


def patch_kernel(tile_rows, tile_cols, nest_rows, ncols, pos, parent, own, kept, g0, g1, g2, g3, out, buf, sems):
    total = nest_rows * SIDE * SIDE
    owns, first_row, begin, aligned, shift, rem_y = window(pos, tile_rows, tile_cols, total)
    my_y = lax.div(lax.axis_index("tiles"), jnp.int32(SIDE))
    ox = pos[0, 0]
    span = SIDE * nest_rows

    @pl.when(owns)
    def _():
        place = (pl.ds(begin, FB_WINDOW), pl.ds(aligned, WIDE))
        buf[...] = kept[...]
        live = rem_y + 3 * lax.broadcasted_iota(jnp.int32, (C, buf.shape[2]), 0) < ncols

        @pl.loop(0, FB_WINDOW)
        def _(w):
            row = first_row + begin + w
            x = 3 * row - ox

            @pl.when((x >= 0) & (x < total))
            def _():
                def from_group(group):
                    r = jnp.clip(row - up_third(ox + span * group), 0, FB_GROUP - 1)
                    return choose(wrap(my_y - group), [ref[r] for ref in (g0, g1, g2, g3)])

                group = lax.div(x, jnp.int32(span))
                value = own[w] + from_group(group)
                spilt = (group > 0) & (x - span * group < STEPS)
                value = value + jnp.where(spilt, from_group(jnp.maximum(group - 1, 0)), 0.0)
                old = buf[w, pl.ds(shift, C), :]
                buf[w, pl.ds(shift, C), :] = jnp.where(live, 0.5 * (old + value), old)

        back = pltpu.make_async_copy(buf, out.at[place], sems.at[0])
        back.start()
        back.wait()


def parent_kernel(
    rows, total, pos, parent, from_up, from_down, west, east, parent_mix, out, kept, token, done, weights, out_sems
):
    height, cols = parent.shape[0], parent.shape[1]
    count, slots = height // rows, done.shape[0]
    owns, _, begin, aligned, _, _ = window(pos, height, cols, total)

    def store(i):
        slot = lax.rem(i, slots)
        return pltpu.make_async_copy(done.at[slot], out.at[pl.ds(i * rows, rows)], out_sems.at[slot])

    size = parent_mix.shape[0]
    weights[...] = wide_weights(parent_mix[...] + jnp.where(eye(size), 1.0 - 4.0 * KAPPA, 0.0))
    index = lax.broadcasted_iota(jnp.int32, (cols, size), 0)
    low_edge, high_edge = index == 0, index == cols - 1

    @pl.loop(0, count)
    def _(i):
        @pl.when(i >= slots)
        def _():
            store(i - slots).wait()

        slot = lax.rem(i, slots)
        for r in range(rows):
            at = i * rows + r
            value = parent[at]
            upper = parent[at - 1] if r else jnp.where(i == 0, from_up[...], parent[jnp.maximum(at - 1, 0)])
            if r < rows - 1:
                lower = parent[at + 1]
            else:
                lower = jnp.where(i == count - 1, from_down[...], parent[jnp.minimum(at + 1, height - 1)])
            left = jnp.where(low_edge, west[pl.ds(at, 1), :], pltpu.roll(value, 1, 0))
            right = jnp.where(high_edge, east[pl.ds(at, 1), :], pltpu.roll(value, cols - 1, 0))
            done[slot, r] = mix(value, weights[...]) + KAPPA * ((upper + lower) + (left + right))
        store(i).start()

        @pl.when(owns & (i * rows < begin + FB_WINDOW) & (i * rows + rows > begin))
        def _():
            for r in range(rows):
                at = i * rows + r - begin

                @pl.when((at >= 0) & (at < FB_WINDOW))
                def _(r=r, at=at):
                    kept[at] = done[slot, r, pl.ds(aligned, WIDE), :]

    for k in range(slots):
        store(count - slots + k).wait()
    token[...] = jnp.zeros(token.shape, F32)


def smem():
    return pl.BlockSpec(memory_space=pltpu.SMEM)


def vmem():
    return pl.BlockSpec(memory_space=pltpu.VMEM)


def hbm():
    return pl.BlockSpec(memory_space=pltpu.HBM)


def run(name, kernel, ins, outs, scratch=(), after=(), room=44, flops=0, moved=1, **options):
    given, held = len(ins), len(after)

    def body(*refs):
        kernel(*refs[:given], *refs[given + held :])

    return pl.pallas_call(
        body,
        out_shape=[shape for _, shape in outs],
        in_specs=[spec for spec, _ in ins] + [pl.BlockSpec(memory_space=pl.ANY)] * held,
        out_specs=[spec for spec, _ in outs],
        scratch_shapes=list(scratch),
        compiler_params=pltpu.CompilerParams(vmem_limit_bytes=room << 20),
        cost_estimate=pl.CostEstimate(flops=flops, bytes_accessed=moved << 20, transcendentals=0),
        name=name,
        **options,
    )(*[value for _, value in ins], *after)


def y_route(k):
    return [(t, (t + SIDE * k) % (SIDE * SIDE)) for t in range(SIDE * SIDE)]


def z_route(k):
    return [(t, t // SIDE * SIDE + (t + k) % SIDE) for t in range(SIDE * SIDE)]


def shards(parent, nest_state, parent_mix, nest_mix, courant, nest_pos):
    tile_rows, tile_cols, width = parent.shape
    state = nest_state[0]
    nest_rows, ncols, _ = state.shape
    total = nest_rows * SIDE * SIDE
    count = SIDE * SIDE
    lines = lax.axis_size("nests")
    S, V, H = smem(), vmem(), hbm()
    big, mid = 52, 44

    def f(*shape):
        return jax.ShapeDtypeStruct(shape, F32)

    def on_tiles(block, route):
        return lax.ppermute(block, "tiles", route)

    packed = run(
        "pack",
        functools.partial(pack_kernel, tile_rows, tile_cols, nest_rows),
        [(S, nest_pos), (H, parent)],
        [(V, f(GROUP_ROWS, C, width))] * SIDE
        + [(V, f(tile_rows, width))] * 2
        + [(V, f(tile_cols, width))] * 2,
        [
            pltpu.VMEM((SIDE, GROUP_ROWS, WIDE, width), F32),
            pltpu.VMEM((2, tile_rows, 8, width), F32),
            pltpu.SemaphoreType.DMA((8,)),
        ],
        room=big,
        moved=4,
    )
    b, (west_out, east_out, down_out, up_out) = packed[:4], packed[4:]
    got = {k: on_tiles(b[k], y_route(k)) for k in (1, 3, 2)}
    from_up = on_tiles(down_out, [(i, i + 1) for i in range(count - 1)])
    from_down = on_tiles(up_out, [(i + 1, i) for i in range(count - 1)])

    fed, tail = run(
        "feed",
        feed_kernel,
        [(S, nest_pos), (V, state), (V, nest_mix), (V, courant)],
        [(V, f(FB_SLOTS, C, width)), (V, f(STEPS, ncols, width))],
        [
            pltpu.VMEM((nest_rows + STEPS, ncols, width), F32),
            pltpu.VMEM((STEPS - 1, nest_rows + STEPS, ncols, width), F32),
        ],
        after=[west_out],
        flops=1 << 28,
        moved=4,
    )
    picked = run(
        "pick",
        functools.partial(pick_kernel, tile_rows, nest_rows),
        [(S, nest_pos)] + [(V, x) for x in (fed, west_out, east_out, b[0], got[1], got[2], got[3])],
        [(V, f(DEV_ROWS + FB_SLOTS, C, width))] * SIDE + [(V, f(tile_rows, width))] * 2,
        after=[from_up, from_down],
    )
    mine = {k: on_tiles(picked[k], z_route(k)) for k in (1, 3, 2)}
    west = lax.ppermute(picked[5], "nests", [(i, i + 1) for i in range(lines - 1)])
    east = lax.ppermute(picked[4], "nests", [(i + 1, i) for i in range(lines - 1)])
    (own,) = run(
        "own_feed",
        functools.partial(own_kernel, tile_rows, tile_cols, total),
        [(S, nest_pos), (H, parent), (V, from_up), (V, nest_mix), (V, courant)],
        [(V, f(FB_WINDOW, C, width))],
        [
            pltpu.VMEM((FB_WINDOW + 1, WIDE + 8, width), F32),
            pltpu.VMEM((FB_WINDOW + 1, C, 4 * width), BF16),
            pltpu.SemaphoreType.DMA((2,)),
        ],
        after=[picked[0]],
        flops=1 << 30,
        moved=8,
    )
    (joined,) = run(
        "combine",
        functools.partial(combine_kernel, nest_rows),
        [(S, nest_pos), (V, picked[0])] + [(V, mine[k]) for k in (1, 2, 3)],
        [(V, f(FB_GROUP, C, width))],
        after=[own],
    )
    groups = {k: on_tiles(joined, y_route(k)) for k in (1, 3, 2)}
    tail, _ = lax.optimization_barrier((tail, joined))
    tail_in = on_tiles(tail, [(i, i + 1) for i in range(count - 1)])

    rows = 8
    parent_new, kept, token = run(
        "parent_step",
        functools.partial(parent_kernel, rows, total),
        [(S, nest_pos), (V, parent)] + [(V, x) for x in (from_up, from_down, west, east, parent_mix)],
        [(H, f(tile_rows, tile_cols, width)), (V, f(FB_WINDOW, WIDE, width)), (V, f(8, width))],
        [
            pltpu.VMEM((4, rows, tile_cols, width), F32),
            pltpu.VMEM((2 * width, 2 * width), BF16),
            pltpu.SemaphoreType.DMA((4,)),
        ],
        after=[joined],
        room=mid,
        flops=2 * tile_rows * tile_cols * 256 * 256,
        moved=10,
    )
    (nest_out,) = run(
        "nest_steps",
        functools.partial(nest_kernel, tile_rows, tile_cols),
        [(S, nest_pos), (V, picked[0])]
        + [(V, mine[k]) for k in (1, 2, 3)]
        + [(V, x) for x in (state, tail_in, nest_mix, courant)],
        [(V, f(nest_rows, ncols, width))],
        [
            pltpu.VMEM((DEV_ROWS, ncols, width), F32),
            pltpu.VMEM((nest_rows + STEPS, ncols, width), F32),
            pltpu.VMEM((STEPS - 1, nest_rows + STEPS, ncols, width), F32),
        ],
        after=[token],
        flops=1 << 28,
        moved=6,
    )
    (parent_out,) = run(
        "patch",
        functools.partial(patch_kernel, tile_rows, tile_cols, nest_rows, ncols),
        [(S, nest_pos), (H, parent_new), (V, own), (V, kept), (V, joined)] + [(V, groups[k]) for k in (1, 2, 3)],
        [(H, f(tile_rows, tile_cols, width))],
        [pltpu.VMEM((FB_WINDOW, WIDE, width), F32), pltpu.SemaphoreType.DMA((1,))],
        room=big,
        moved=2,
        input_output_aliases={1: 0},
    )
    return parent_out, nest_out[None]


def solution(mesh):
    placed = (
        P("tiles", "nests", None),
        P("nests", "tiles", None, None),
        P(),
        P(),
        P(),
        P("nests", None),
    )
    return jax.shard_map(
        shards,
        mesh=mesh,
        in_specs=placed,
        out_specs=(P("tiles", "nests", None), P("nests", "tiles", None, None)),
        check_vma=False,
    )
```

```python
import functools

import jax
import jax.numpy as jnp
from jax import lax
from jax.experimental import pallas as pl
from jax.experimental.pallas import tpu as pltpu
from jax.sharding import PartitionSpec as P

STEPS = 3
KAPPA = 0.125
C = 48
WIDE = 56
SIDE = 4
GROUP_ROWS = 8
DEV_ROWS = 4
FB_SLOTS = 3
FB_GROUP = 7
FB_WINDOW = 22
F32 = jnp.float32
BF16 = jnp.bfloat16


def third(value):
    return lax.div(value, jnp.int32(3))


def wrap(value):
    return lax.rem(value + 2 * SIDE, jnp.int32(SIDE))


def split(value):
    high = value.astype(BF16)
    return high, (value - high.astype(F32)).astype(BF16)


def wide_weights(matrix):
    high, low = split(matrix)
    row = jnp.concatenate([high, low], axis=1)
    return jnp.concatenate([row, row], axis=0)


def mix(value, weights):
    lhs = jnp.concatenate(split(value), axis=1)
    both = jnp.dot(lhs, weights, preferred_element_type=F32)
    half = both.shape[1] // 2
    return both[:, :half] + both[:, half:]


def choose(way, values):
    result = values[-1]
    for k in range(len(values) - 2, -1, -1):
        result = jnp.where(way == k, values[k], result)
    return result


def eye(size):
    shape = (size, size)
    return lax.broadcasted_iota(jnp.int32, shape, 0) == lax.broadcasted_iota(jnp.int32, shape, 1)


def nest_weights(nest_mix, courant):
    c0, c1 = courant[0:1, :], courant[1:2, :]
    stay = jnp.where(eye(nest_mix.shape[0]), 1.0 - c0 - c1, 0.0)
    return c0, c1, wide_weights(nest_mix[...] + stay)


def owner_place(row, first, tile_rows):
    owner = lax.div(jnp.maximum(row, 0), jnp.int32(tile_rows))
    base = owner * tile_rows
    begin = jnp.clip(first - base, 0, tile_rows - GROUP_ROWS)
    return owner, jnp.clip(row - base - begin, 0, GROUP_ROWS - 1)


def pack_kernel(tile_rows, tile_cols, nest_rows, pos, parent, b0, b1, b2, b3, west, east, down, up, band, cols, sems):
    tile = lax.axis_index("tiles")
    line = lax.axis_index("nests")
    my_y = lax.div(tile, jnp.int32(SIDE))
    corner = third(pos[0, 1]) - line * tile_cols
    aligned = pl.multiple_of(lax.div(corner, jnp.int32(8)) * 8, 8)
    shift = corner - aligned
    copies = []
    for k in range(SIDE):
        group = wrap(my_y + k)
        first = third(pos[0, 0] + SIDE * nest_rows * group) - 1
        begin = jnp.clip(first - tile * tile_rows, 0, tile_rows - GROUP_ROWS)
        copies.append(
            pltpu.make_async_copy(
                parent.at[pl.ds(begin, GROUP_ROWS), pl.ds(aligned, WIDE)], band.at[k], sems.at[k]
            )
        )
    others = [
        pltpu.make_async_copy(parent.at[:, pl.ds(0, 8)], cols.at[0], sems.at[4]),
        pltpu.make_async_copy(parent.at[:, pl.ds(tile_cols - 8, 8)], cols.at[1], sems.at[5]),
        pltpu.make_async_copy(parent.at[tile_rows - 1], down, sems.at[6]),
        pltpu.make_async_copy(parent.at[0], up, sems.at[7]),
    ]
    for copy in copies + others:
        copy.start()
    for k, out in enumerate((b0, b1, b2, b3)):
        copies[k].wait()
        for r in range(GROUP_ROWS):
            out[r] = band[k, r, pl.ds(shift, C), :]
    others[0].wait()
    west[...] = cols[0, :, 0, :]
    others[1].wait()
    east[...] = cols[1, :, 7, :]
    for copy in others[2:]:
        copy.wait()


def pick_kernel(tile_rows, nest_rows, pos, fed, r0, r1, r2, r3, o0, o1, o2, o3):
    tile = lax.axis_index("tiles")
    my_y, my_z = lax.div(tile, jnp.int32(SIDE)), lax.rem(tile, jnp.int32(SIDE))
    first = third(pos[0, 0] + SIDE * nest_rows * my_y) - 1
    for k, out in enumerate((o0, o1, o2, o3)):
        target = my_y * SIDE + wrap(my_z + k)
        top = third(pos[0, 0] + nest_rows * target) - 1
        for j in range(DEV_ROWS):
            owner, place = owner_place(top + j, first, tile_rows)
            way = wrap(my_y - lax.div(owner, jnp.int32(SIDE)))
            out[j] = choose(way, [ref[place] for ref in (r0, r1, r2, r3)])
        for s in range(FB_SLOTS):
            out[DEV_ROWS + s] = fed[s]


def nest_kernel(tile_rows, tile_cols, pos, r0, r1, r2, r3, state, tail, nest_mix, courant, out, token, lines, start, cur):
    tile = lax.axis_index("tiles")
    my_y, my_z = lax.div(tile, jnp.int32(SIDE)), lax.rem(tile, jnp.int32(SIDE))
    nest_rows, ncols, width = state.shape
    halo = STEPS
    ox, oy = pos[0, 0], pos[0, 1]
    phase = lax.rem(oy, jnp.int32(3))
    top = third(ox + nest_rows * tile) - 1
    spot = lax.broadcasted_iota(jnp.int32, (ncols, C), 0) + phase
    near = third(spot)
    frac = spot - 3 * near
    place = lax.broadcasted_iota(jnp.int32, (ncols, C), 1)
    table = jnp.where(place == near, 3 - frac, jnp.where(place == near + 1, frac, 0))
    table = table.astype(F32).astype(BF16)
    for j in range(DEV_ROWS):
        owner = lax.div(jnp.maximum(top + j, 0), jnp.int32(tile_rows))
        way = wrap(my_z - lax.rem(owner, jnp.int32(SIDE)))
        high, low = split(choose(way, [ref[j] for ref in (r0, r1, r2, r3)]))
        lines[j] = jnp.dot(table, high, preferred_element_type=F32) + jnp.dot(
            table, low, preferred_element_type=F32
        )
    for x in range(-halo, nest_rows):
        at = ox + nest_rows * tile + x
        at = jnp.maximum(at, 0)
        near_row = jnp.clip(third(at) - top, 0, DEV_ROWS - 2)
        part = lax.rem(at, jnp.int32(3)).astype(F32)
        interp = (3.0 - part) * lines[near_row] + part * lines[near_row + 1]
        own = state[x] if x >= 0 else tail[x + halo]
        start[x + halo] = 0.5 * (own + interp * (1.0 / 9.0))
    first = tile == 0

    @pl.when(first)
    def _():
        for x in range(halo):
            start[x] = start[halo]

    c0, c1, weights = nest_weights(nest_mix, courant)
    edge_row = lax.broadcasted_iota(jnp.int32, (ncols, width), 0) == 0
    source = start
    for step in range(STEPS):
        last = step == STEPS - 1
        for r in range(nest_rows + halo - 1, step, -1):
            value = source[r]
            left = jnp.where(edge_row, start[r, 0:1, :], pltpu.roll(value, 1, 0))
            value = mix(value, weights) + c0 * source[r - 1] + c1 * left
            if r < halo:
                value = jnp.where(first, start[halo], value)
            if last:
                out[r - halo] = value
            else:
                cur[step, r] = value
        source = cur.at[step]
    token[...] = jnp.zeros(token.shape, F32)


def up_third(value):
    return third(value + 2)


def feed_kernel(pos, state, nest_mix, courant, fb, tail, mix_out, start, cur):
    tile = lax.axis_index("tiles")
    nest_rows, ncols, width = state.shape
    rows = nest_rows + STEPS
    ox, oy = pos[0, 0], pos[0, 1]
    tail[...] = state[nest_rows - STEPS :]
    mix_out[...] = nest_mix[...]
    for x in range(rows):
        start[x] = 0.5 * state[x] if x < nest_rows else jnp.zeros((ncols, width), F32)
    above = jnp.where(tile == 0, start[0], 0.0)
    c0, c1, weights = nest_weights(nest_mix, courant)
    edge_row = lax.broadcasted_iota(jnp.int32, (ncols, width), 0) == 0

    def advanced(value, upper, edge):
        left = jnp.where(edge_row, edge, pltpu.roll(value, 1, 0))
        return mix(value, weights) + c0 * upper + c1 * left

    source = start
    for step in range(STEPS - 1):
        for r in range(nest_rows + step + 1):
            upper = above if r == 0 else source[r - 1]
            cur[step, r] = advanced(source[r], upper, start[r, 0:1, :])
        for r in range(nest_rows + step + 1, rows):
            cur[step, r] = jnp.zeros((ncols, width), F32)
        source = cur.at[step]
    rem_y = lax.rem(3 - lax.rem(oy, jnp.int32(3)), jnp.int32(3))
    slot = lax.broadcasted_iota(jnp.int32, (C, ncols), 0)
    pick = (lax.broadcasted_iota(jnp.int32, (C, ncols), 1) == rem_y + 3 * slot).astype(F32).astype(BF16)
    pick = jnp.concatenate([pick, pick], axis=1)
    first = up_third(ox + nest_rows * tile) * 3 - ox - nest_rows * tile
    for s in range(FB_SLOTS):
        r = jnp.minimum(first + 3 * s, rows - 1)
        upper = source[jnp.maximum(r - 1, 0)]
        if s == 0:
            upper = jnp.where(r == 0, above, upper)
        value = advanced(source[r], upper, start[r, 0:1, :])
        fb[s] = jnp.dot(pick, jnp.concatenate(split(value), axis=0), preferred_element_type=F32)


def combine_kernel(nest_rows, pos, e0, e1, e2, e3, out):
    tile = lax.axis_index("tiles")
    my_y, my_z = lax.div(tile, jnp.int32(SIDE)), lax.rem(tile, jnp.int32(SIDE))
    ox = pos[0, 0]
    base = up_third(ox + SIDE * nest_rows * my_y)
    for r in range(FB_GROUP):
        out[r] = jnp.zeros(out.shape[1:], F32)
    for k, ref in enumerate((e0, e1, e2, e3)):
        origin = ox + nest_rows * (SIDE * my_y + wrap(my_z - k))
        row = up_third(origin)
        for s in range(FB_SLOTS):

            @pl.when(3 * (row + s) - origin < nest_rows + STEPS)
            def _(ref=ref, row=row, s=s):
                out[row + s - base] += ref[DEV_ROWS + s]


def window(pos, tile_rows, tile_cols, total):
    ox, oy = pos[0, 0], pos[0, 1]
    first_row = lax.axis_index("tiles") * tile_rows
    low_row, high_row = up_third(ox), third(ox + total - 1)
    owns = (high_row >= first_row) & (low_row < first_row + tile_rows)
    begin = jnp.clip(low_row - first_row, 0, tile_rows - FB_WINDOW)
    corner = third(oy) - lax.axis_index("nests") * tile_cols
    aligned = pl.multiple_of(lax.div(corner, jnp.int32(8)) * 8, 8)
    shift = corner - aligned + up_third(oy) - third(oy)
    return owns, first_row, begin, aligned, shift, up_third(oy) * 3 - oy


def own_kernel(tile_rows, tile_cols, total, pos, parent, from_up, nest_mix, courant, out, buf, parts, sems):
    owns, first_row, begin, aligned, shift, rem_y = window(pos, tile_rows, tile_cols, total)
    ox = pos[0, 0]
    width = buf.shape[2]

    @pl.when(owns)
    def _():
        cols = pl.ds(aligned, WIDE)
        main = pltpu.make_async_copy(
            parent.at[pl.ds(begin, FB_WINDOW), cols], buf.at[pl.ds(1, FB_WINDOW), pl.ds(8, WIDE)], sems.at[0]
        )
        edge = pltpu.make_async_copy(
            parent.at[jnp.maximum(begin - 1, 0), cols], buf.at[0, pl.ds(8, WIDE)], sems.at[1]
        )
        main.start()
        edge.start()
        buf[:, 0:8, :] = jnp.zeros((FB_WINDOW + 1, 8, width), F32)

        c0, c1 = courant[0:1, :], courant[1:2, :]
        diagonal = eye(width)
        r0 = jnp.sum(jnp.where(diagonal, c0, 0.0), axis=1, keepdims=True)
        r1 = jnp.sum(jnp.where(diagonal, c1, 0.0), axis=1, keepdims=True)
        one = nest_mix[...] + jnp.where(diagonal, 1.0 - c0 - c1, 0.0)
        weights = wide_weights(one)
        many = mix(jnp.concatenate([one, one * c0, one * c1], axis=0), weights)
        two, by0, by1 = many[:width], many[width : 2 * width], many[2 * width :]
        paths = {
            (0, 0): mix(two, weights),
            (1, 0): r0 * two + by0 + two * c0,
            (0, 1): r1 * two + by1 + two * c1,
            (2, 0): (r0 * r0) * one + (r0 * one) * c0 + one * (c0 * c0),
            (0, 2): (r1 * r1) * one + (r1 * one) * c1 + one * (c1 * c1),
            (1, 1): (2.0 * r0 * r1) * one + (r0 * one) * c1 + (r1 * one) * c0 + one * (2.0 * c0 * c1),
            (3, 0): jnp.where(diagonal, c0 * c0 * c0, 0.0),
            (0, 3): jnp.where(diagonal, c1 * c1 * c1, 0.0),
            (2, 1): jnp.where(diagonal, 3.0 * c0 * c0 * c1, 0.0),
            (1, 2): jnp.where(diagonal, 3.0 * c0 * c1 * c1, 0.0),
        }

        def corner(low_row, low_col):
            sum_of = jnp.zeros((width, width), F32)
            for (i, j), path in paths.items():
                weight = (i if low_row else 3 - i) * (j if low_col else 3 - j) * (0.5 / 9.0)
                if weight:
                    sum_of = sum_of + weight * path
            return wide_weights(sum_of)

        this_row = jnp.concatenate([corner(False, False), corner(False, True)], axis=0)
        row_before = jnp.concatenate([corner(True, False), corner(True, True)], axis=0)

        main.wait()
        edge.wait()

        @pl.when(begin == 0)
        def _():
            buf[0, pl.ds(8, WIDE), :] = from_up[pl.ds(aligned, WIDE), :]

        for w in range(FB_WINDOW + 1):
            near = buf[w, pl.ds(8 + shift, C), :]
            back = buf[w, pl.ds(7 + shift, C), :]
            parts[w] = jnp.concatenate(split(near) + split(back), axis=1)
        batch = FB_WINDOW // 2
        for w in range(0, FB_WINDOW, batch):
            this = parts[w + 1 : w + 1 + batch].reshape(batch * C, 4 * width)
            before = parts[w : w + batch].reshape(batch * C, 4 * width)
            both = jnp.dot(this, this_row, preferred_element_type=F32) + jnp.dot(
                before, row_before, preferred_element_type=F32
            )
            out[w : w + batch] = (both[:, :width] + both[:, width:]).reshape(batch, C, width)

        first = up_third(ox) - first_row - begin
        at = jnp.clip(first, 0, FB_WINDOW - 1)
        pad = jnp.zeros((24 - FB_WINDOW, width), F32)

        def gather(k, offset):
            column = buf[pl.ds(k, FB_WINDOW), pl.ds(offset + shift, 1), :].reshape(FB_WINDOW, width)
            return jnp.concatenate([buf[at + k, pl.ds(offset + shift, C), :], column, pad], axis=0)

        near = [gather(k, 8) for k in range(2)]
        back = [gather(k, 7) for k in range(2)]
        line = lax.broadcasted_iota(jnp.int32, near[0].shape, 0)
        in_row = line < C
        x = 3 * (first_row + begin + jnp.where(in_row, at, line - C)) - ox
        y = rem_y + 3 * jnp.where(in_row, line, 0)
        start = {}
        for i in range(STEPS + 1):
            lean = jnp.minimum(x, i).astype(F32) * (0.5 / 9.0)
            rest = 0.5 / 3.0 - lean
            right = rest * near[1] + lean * near[0]
            left = rest * back[1] + lean * back[0]
            for j in range(STEPS + 1 - i):
                tilt = jnp.minimum(y, j).astype(F32)
                start[i, j] = right * (3.0 - tilt) + left * tilt
        cells = start
        size = C + 24
        for step in range(STEPS):
            keys = [(i, j) for i in range(STEPS - step) for j in range(STEPS - step - i)]
            mixed = mix(jnp.concatenate([cells[key] for key in keys], axis=0), weights)
            fresh = {}
            for n, (i, j) in enumerate(keys):
                value = mixed[n * size : (n + 1) * size] + c0 * cells[i + 1, j] + c1 * cells[i, j + 1]
                fresh[i, j] = jnp.where((x < i) | (y < j), start[i, j], value)
            cells = fresh
        edges = cells[0, 0]

        @pl.when((first >= 0) & (first < FB_WINDOW))
        def _():
            out[at] = edges[:C]

        for w in range(FB_WINDOW):
            out[w, 0:1, :] = edges[C + w : C + w + 1]


def patch_kernel(tile_rows, tile_cols, nest_rows, ncols, pos, parent, own, kept, g0, g1, g2, g3, out, buf, sems):
    total = nest_rows * SIDE * SIDE
    owns, first_row, begin, aligned, shift, rem_y = window(pos, tile_rows, tile_cols, total)
    my_y = lax.div(lax.axis_index("tiles"), jnp.int32(SIDE))
    ox = pos[0, 0]
    span = SIDE * nest_rows

    @pl.when(owns)
    def _():
        place = (pl.ds(begin, FB_WINDOW), pl.ds(aligned, WIDE))
        buf[...] = kept[...]
        live = rem_y + 3 * lax.broadcasted_iota(jnp.int32, (C, buf.shape[2]), 0) < ncols

        @pl.loop(0, FB_WINDOW)
        def _(w):
            row = first_row + begin + w
            x = 3 * row - ox

            @pl.when((x >= 0) & (x < total))
            def _():
                def from_group(group):
                    r = jnp.clip(row - up_third(ox + span * group), 0, FB_GROUP - 1)
                    return choose(wrap(my_y - group), [ref[r] for ref in (g0, g1, g2, g3)])

                group = lax.div(x, jnp.int32(span))
                value = own[w] + from_group(group)
                spilt = (group > 0) & (x - span * group < STEPS)
                value = value + jnp.where(spilt, from_group(jnp.maximum(group - 1, 0)), 0.0)
                old = buf[w, pl.ds(shift, C), :]
                buf[w, pl.ds(shift, C), :] = jnp.where(live, 0.5 * (old + value), old)

        back = pltpu.make_async_copy(buf, out.at[place], sems.at[0])
        back.start()
        back.wait()


def parent_kernel(
    rows, total, tiles, lines, pos, parent, from_up, from_down, west, east, parent_mix, out, kept, token, done, weights, out_sems
):
    height, cols = parent.shape[0], parent.shape[1]
    count, slots = height // rows, done.shape[0]
    owns, _, begin, aligned, _, _ = window(pos, height, cols, total)
    tile, line = lax.axis_index("tiles"), lax.axis_index("nests")

    def store(i):
        slot = lax.rem(i, slots)
        return pltpu.make_async_copy(done.at[slot], out.at[pl.ds(i * rows, rows)], out_sems.at[slot])

    size = parent_mix.shape[0]
    weights[...] = wide_weights(parent_mix[...] + jnp.where(eye(size), 1.0 - 4.0 * KAPPA, 0.0))
    index = lax.broadcasted_iota(jnp.int32, (cols, size), 0)
    low_edge, high_edge = index == 0, index == cols - 1

    @pl.loop(0, count)
    def _(i):
        @pl.when(i >= slots)
        def _():
            store(i - slots).wait()

        slot = lax.rem(i, slots)
        for r in range(rows):
            at = i * rows + r
            value = parent[at]
            upper = parent[at - 1] if r else jnp.where(i == 0, jnp.where(tile > 0, from_up[...], 0.0), parent[jnp.maximum(at - 1, 0)])
            if r < rows - 1:
                lower = parent[at + 1]
            else:
                lower = jnp.where(
                    i == count - 1, jnp.where(tile < tiles - 1, from_down[...], 0.0), parent[jnp.minimum(at + 1, height - 1)]
                )
            left = jnp.where(low_edge, jnp.where(line > 0, west[pl.ds(at, 1), :], 0.0), pltpu.roll(value, 1, 0))
            right = jnp.where(
                high_edge, jnp.where(line < lines - 1, east[pl.ds(at, 1), :], 0.0), pltpu.roll(value, cols - 1, 0)
            )
            done[slot, r] = mix(value, weights[...]) + KAPPA * ((upper + lower) + (left + right))
        store(i).start()

        @pl.when(owns & (i * rows < begin + FB_WINDOW) & (i * rows + rows > begin))
        def _():
            for r in range(rows):
                at = i * rows + r - begin

                @pl.when((at >= 0) & (at < FB_WINDOW))
                def _(r=r, at=at):
                    kept[at] = done[slot, r, pl.ds(aligned, WIDE), :]

    for k in range(slots):
        store(count - slots + k).wait()
    token[...] = jnp.zeros(token.shape, F32)


def smem():
    return pl.BlockSpec(memory_space=pltpu.SMEM)


def vmem():
    return pl.BlockSpec(memory_space=pltpu.VMEM)


def hbm():
    return pl.BlockSpec(memory_space=pltpu.HBM)


def run(name, kernel, ins, outs, scratch=(), after=(), room=44, flops=0, moved=1, **options):
    given, held = len(ins), len(after)

    def body(*refs):
        kernel(*refs[:given], *refs[given + held :])

    return pl.pallas_call(
        body,
        out_shape=[shape for _, shape in outs],
        in_specs=[spec for spec, _ in ins] + [pl.BlockSpec(memory_space=pl.ANY)] * held,
        out_specs=[spec for spec, _ in outs],
        scratch_shapes=list(scratch),
        compiler_params=pltpu.CompilerParams(vmem_limit_bytes=room << 20),
        cost_estimate=pl.CostEstimate(flops=flops, bytes_accessed=moved << 20, transcendentals=0),
        name=name,
        **options,
    )(*[value for _, value in ins], *after)


def around(count, step):
    return [(i, (i + step) % count) for i in range(count)]


def y_route(k):
    return [(t, (t + SIDE * k) % (SIDE * SIDE)) for t in range(SIDE * SIDE)]


def z_route(k):
    return [(t, t // SIDE * SIDE + (t + k) % SIDE) for t in range(SIDE * SIDE)]


def shards(parent, nest_state, parent_mix, nest_mix, courant, nest_pos):
    tile_rows, tile_cols, width = parent.shape
    state = nest_state[0]
    nest_rows, ncols, _ = state.shape
    total = nest_rows * SIDE * SIDE
    count = SIDE * SIDE
    lines = lax.axis_size("nests")
    S, V, H = smem(), vmem(), hbm()
    big, mid = 52, 44

    def f(*shape):
        return jax.ShapeDtypeStruct(shape, F32)

    def on_tiles(block, route):
        return lax.ppermute(block, "tiles", route)

    packed = run(
        "pack",
        functools.partial(pack_kernel, tile_rows, tile_cols, nest_rows),
        [(S, nest_pos), (H, parent)],
        [(V, f(GROUP_ROWS, C, width))] * SIDE
        + [(V, f(tile_rows, width))] * 2
        + [(V, f(tile_cols, width))] * 2,
        [
            pltpu.VMEM((SIDE, GROUP_ROWS, WIDE, width), F32),
            pltpu.VMEM((2, tile_rows, 8, width), F32),
            pltpu.SemaphoreType.DMA((8,)),
        ],
        room=big,
        moved=4,
    )
    b, (west_out, east_out, down_out, up_out) = packed[:4], packed[4:]
    got = {k: on_tiles(b[k], y_route(k)) for k in (1, 3, 2)}
    from_up = on_tiles(down_out, around(count, 1))
    from_down = on_tiles(up_out, around(count, -1))

    fed, tail, mix_kept = run(
        "feed",
        feed_kernel,
        [(S, nest_pos), (V, state), (V, nest_mix), (V, courant)],
        [(V, f(FB_SLOTS, C, width)), (V, f(STEPS, ncols, width)), (V, f(width, width))],
        [
            pltpu.VMEM((nest_rows + STEPS, ncols, width), F32),
            pltpu.VMEM((STEPS - 1, nest_rows + STEPS, ncols, width), F32),
        ],
        after=[west_out],
        flops=1 << 28,
        moved=4,
    )
    east_out, west_out, _ = lax.optimization_barrier((east_out, west_out, fed))
    west = lax.ppermute(east_out, "nests", around(lines, 1))
    east = lax.ppermute(west_out, "nests", around(lines, -1))
    picked = run(
        "pick",
        functools.partial(pick_kernel, tile_rows, nest_rows),
        [(S, nest_pos)] + [(V, x) for x in (fed, b[0], got[1], got[2], got[3])],
        [(V, f(DEV_ROWS + FB_SLOTS, C, width))] * SIDE,
        after=[from_down],
    )
    mine = {k: on_tiles(picked[k], z_route(k)) for k in (1, 3, 2)}
    tail, _ = lax.optimization_barrier((tail, picked[1]))
    tail_in = on_tiles(tail, around(count, 1))

    (own,) = run(
        "own_feed",
        functools.partial(own_kernel, tile_rows, tile_cols, total),
        [(S, nest_pos), (H, parent), (V, from_up), (V, mix_kept), (V, courant)],
        [(V, f(FB_WINDOW, C, width))],
        [
            pltpu.VMEM((FB_WINDOW + 1, WIDE + 8, width), F32),
            pltpu.VMEM((FB_WINDOW + 1, C, 4 * width), BF16),
            pltpu.SemaphoreType.DMA((2,)),
        ],
        after=[picked[0]],
        flops=1 << 30,
        moved=8,
    )
    rows = 8
    parent_new, kept, token = run(
        "parent_step",
        functools.partial(parent_kernel, rows, total, count, lines),
        [(S, nest_pos), (V, parent)] + [(V, x) for x in (from_up, from_down, west, east, parent_mix)],
        [(H, f(tile_rows, tile_cols, width)), (V, f(FB_WINDOW, WIDE, width)), (V, f(8, width))],
        [
            pltpu.VMEM((4, rows, tile_cols, width), F32),
            pltpu.VMEM((2 * width, 2 * width), BF16),
            pltpu.SemaphoreType.DMA((4,)),
        ],
        after=[own],
        room=mid,
        flops=2 * tile_rows * tile_cols * 256 * 256,
        moved=10,
    )
    (joined,) = run(
        "combine",
        functools.partial(combine_kernel, nest_rows),
        [(S, nest_pos), (V, picked[0])] + [(V, mine[k]) for k in (1, 2, 3)],
        [(V, f(FB_GROUP, C, width))],
        after=[token],
    )
    groups = {k: on_tiles(joined, y_route(k)) for k in (1, 3, 2)}

    nest_out, moved_on = run(
        "nest_steps",
        functools.partial(nest_kernel, tile_rows, tile_cols),
        [(S, nest_pos), (V, picked[0])]
        + [(V, mine[k]) for k in (1, 2, 3)]
        + [(V, x) for x in (state, tail_in, mix_kept, courant)],
        [(V, f(nest_rows, ncols, width)), (V, f(8, width))],
        [
            pltpu.VMEM((DEV_ROWS, ncols, width), F32),
            pltpu.VMEM((nest_rows + STEPS, ncols, width), F32),
            pltpu.VMEM((STEPS - 1, nest_rows + STEPS, ncols, width), F32),
        ],
        after=[joined],
        flops=1 << 28,
        moved=6,
    )
    (parent_out,) = run(
        "patch",
        functools.partial(patch_kernel, tile_rows, tile_cols, nest_rows, ncols),
        [(S, nest_pos), (H, parent_new), (V, own), (V, kept), (V, joined)] + [(V, groups[k]) for k in (1, 2, 3)],
        [(H, f(tile_rows, tile_cols, width))],
        [pltpu.VMEM((FB_WINDOW, WIDE, width), F32), pltpu.SemaphoreType.DMA((1,))],
        room=big,
        moved=2,
        input_output_aliases={1: 0},
    )
    return parent_out, nest_out[None]


def solution(mesh):
    placed = (
        P("tiles", "nests", None),
        P("nests", "tiles", None, None),
        P(),
        P(),
        P(),
        P("nests", None),
    )
    return jax.shard_map(
        shards,
        mesh=mesh,
        in_specs=placed,
        out_specs=(P("tiles", "nests", None), P("nests", "tiles", None, None)),
        check_vma=False,
    )
```

```python
import functools

import jax
import jax.numpy as jnp
from jax import lax
from jax.experimental import pallas as pl
from jax.experimental.pallas import tpu as pltpu
from jax.sharding import PartitionSpec as P

STEPS = 3
KAPPA = 0.125
C = 48
WIDE = 56
SIDE = 4
GROUP_ROWS = 8
DEV_ROWS = 4
FB_SLOTS = 3
FB_GROUP = 7
FB_WINDOW = 22
F32 = jnp.float32
BF16 = jnp.bfloat16


def third(value):
    return lax.div(value, jnp.int32(3))


def wrap(value):
    return lax.rem(value + 2 * SIDE, jnp.int32(SIDE))


def split(value):
    high = value.astype(BF16)
    return high, (value - high.astype(F32)).astype(BF16)


def wide_weights(matrix):
    high, low = split(matrix)
    row = jnp.concatenate([high, low], axis=1)
    return jnp.concatenate([row, row], axis=0)


def mix(value, weights):
    lhs = jnp.concatenate(split(value), axis=1)
    both = jnp.dot(lhs, weights, preferred_element_type=F32)
    half = both.shape[1] // 2
    return both[:, :half] + both[:, half:]


def choose(way, values):
    result = values[-1]
    for k in range(len(values) - 2, -1, -1):
        result = jnp.where(way == k, values[k], result)
    return result


def eye(size):
    shape = (size, size)
    return lax.broadcasted_iota(jnp.int32, shape, 0) == lax.broadcasted_iota(jnp.int32, shape, 1)


def nest_weights(nest_mix, courant):
    c0, c1 = courant[0:1, :], courant[1:2, :]
    stay = jnp.where(eye(nest_mix.shape[0]), 1.0 - c0 - c1, 0.0)
    return c0, c1, wide_weights(nest_mix[...] + stay)


def owner_place(row, first, tile_rows):
    owner = lax.div(jnp.maximum(row, 0), jnp.int32(tile_rows))
    base = owner * tile_rows
    begin = jnp.clip(first - base, 0, tile_rows - GROUP_ROWS)
    return owner, jnp.clip(row - base - begin, 0, GROUP_ROWS - 1)


def pack_kernel(tile_rows, tile_cols, nest_rows, pos, parent, b0, b1, b2, b3, west, east, down, up, band, cols, sems):
    tile = lax.axis_index("tiles")
    line = lax.axis_index("nests")
    my_y = lax.div(tile, jnp.int32(SIDE))
    corner = third(pos[0, 1]) - line * tile_cols
    aligned = pl.multiple_of(lax.div(corner, jnp.int32(8)) * 8, 8)
    shift = corner - aligned
    copies = []
    for k in range(SIDE):
        group = wrap(my_y + k)
        first = third(pos[0, 0] + SIDE * nest_rows * group) - 1
        begin = jnp.clip(first - tile * tile_rows, 0, tile_rows - GROUP_ROWS)
        copies.append(
            pltpu.make_async_copy(
                parent.at[pl.ds(begin, GROUP_ROWS), pl.ds(aligned, WIDE)], band.at[k], sems.at[k]
            )
        )
    others = [
        pltpu.make_async_copy(parent.at[:, pl.ds(0, 8)], cols.at[0], sems.at[4]),
        pltpu.make_async_copy(parent.at[:, pl.ds(tile_cols - 8, 8)], cols.at[1], sems.at[5]),
        pltpu.make_async_copy(parent.at[tile_rows - 1], down, sems.at[6]),
        pltpu.make_async_copy(parent.at[0], up, sems.at[7]),
    ]
    for copy in copies + others:
        copy.start()
    for k, out in enumerate((b0, b1, b2, b3)):
        copies[k].wait()
        for r in range(GROUP_ROWS):
            out[r] = band[k, r, pl.ds(shift, C), :]
    others[0].wait()
    west[...] = cols[0, :, 0, :]
    others[1].wait()
    east[...] = cols[1, :, 7, :]
    for copy in others[2:]:
        copy.wait()


def pick_kernel(tile_rows, nest_rows, pos, fed, r0, r1, r2, r3, o0, o1, o2, o3):
    tile = lax.axis_index("tiles")
    my_y, my_z = lax.div(tile, jnp.int32(SIDE)), lax.rem(tile, jnp.int32(SIDE))
    first = third(pos[0, 0] + SIDE * nest_rows * my_y) - 1
    for k, out in enumerate((o0, o1, o2, o3)):
        target = my_y * SIDE + wrap(my_z + k)
        top = third(pos[0, 0] + nest_rows * target) - 1
        for j in range(DEV_ROWS):
            owner, place = owner_place(top + j, first, tile_rows)
            way = wrap(my_y - lax.div(owner, jnp.int32(SIDE)))
            out[j] = choose(way, [ref[place] for ref in (r0, r1, r2, r3)])
        for s in range(FB_SLOTS):
            out[DEV_ROWS + s] = fed[s]


def nest_kernel(tile_rows, tile_cols, pos, r0, r1, r2, r3, state, tail, nest_mix, courant, out, token, lines, start, cur):
    tile = lax.axis_index("tiles")
    my_y, my_z = lax.div(tile, jnp.int32(SIDE)), lax.rem(tile, jnp.int32(SIDE))
    nest_rows, ncols, width = state.shape
    halo = STEPS
    ox, oy = pos[0, 0], pos[0, 1]
    phase = lax.rem(oy, jnp.int32(3))
    top = third(ox + nest_rows * tile) - 1
    spot = lax.broadcasted_iota(jnp.int32, (ncols, C), 0) + phase
    near = third(spot)
    frac = spot - 3 * near
    place = lax.broadcasted_iota(jnp.int32, (ncols, C), 1)
    table = jnp.where(place == near, 3 - frac, jnp.where(place == near + 1, frac, 0))
    table = table.astype(F32).astype(BF16)
    for j in range(DEV_ROWS):
        owner = lax.div(jnp.maximum(top + j, 0), jnp.int32(tile_rows))
        way = wrap(my_z - lax.rem(owner, jnp.int32(SIDE)))
        high, low = split(choose(way, [ref[j] for ref in (r0, r1, r2, r3)]))
        lines[j] = jnp.dot(table, high, preferred_element_type=F32) + jnp.dot(
            table, low, preferred_element_type=F32
        )
    for x in range(-halo, nest_rows):
        at = ox + nest_rows * tile + x
        at = jnp.maximum(at, 0)
        near_row = jnp.clip(third(at) - top, 0, DEV_ROWS - 2)
        part = lax.rem(at, jnp.int32(3)).astype(F32)
        interp = (3.0 - part) * lines[near_row] + part * lines[near_row + 1]
        own = state[x] if x >= 0 else tail[x + halo]
        start[x + halo] = 0.5 * (own + interp * (1.0 / 9.0))
    first = tile == 0

    @pl.when(first)
    def _():
        for x in range(halo):
            start[x] = start[halo]

    c0, c1, weights = nest_weights(nest_mix, courant)
    edge_row = lax.broadcasted_iota(jnp.int32, (ncols, width), 0) == 0
    source = start
    for step in range(STEPS):
        last = step == STEPS - 1
        for r in range(nest_rows + halo - 1, step, -1):
            value = source[r]
            left = jnp.where(edge_row, start[r, 0:1, :], pltpu.roll(value, 1, 0))
            value = mix(value, weights) + c0 * source[r - 1] + c1 * left
            if r < halo:
                value = jnp.where(first, start[halo], value)
            if last:
                out[r - halo] = value
            else:
                cur[step, r] = value
        source = cur.at[step]
    token[...] = jnp.zeros(token.shape, F32)


def up_third(value):
    return third(value + 2)


def feed_kernel(pos, state, nest_mix, courant, fb, tail, mix_out, start, cur):
    tile = lax.axis_index("tiles")
    nest_rows, ncols, width = state.shape
    rows = nest_rows + STEPS
    ox, oy = pos[0, 0], pos[0, 1]
    tail[...] = state[nest_rows - STEPS :]
    mix_out[...] = nest_mix[...]
    for x in range(rows):
        start[x] = 0.5 * state[x] if x < nest_rows else jnp.zeros((ncols, width), F32)
    above = jnp.where(tile == 0, start[0], 0.0)
    c0, c1, weights = nest_weights(nest_mix, courant)
    edge_row = lax.broadcasted_iota(jnp.int32, (ncols, width), 0) == 0

    def advanced(value, upper, edge):
        left = jnp.where(edge_row, edge, pltpu.roll(value, 1, 0))
        return mix(value, weights) + c0 * upper + c1 * left

    source = start
    for step in range(STEPS - 1):
        for r in range(nest_rows + step + 1):
            upper = above if r == 0 else source[r - 1]
            cur[step, r] = advanced(source[r], upper, start[r, 0:1, :])
        for r in range(nest_rows + step + 1, rows):
            cur[step, r] = jnp.zeros((ncols, width), F32)
        source = cur.at[step]
    rem_y = lax.rem(3 - lax.rem(oy, jnp.int32(3)), jnp.int32(3))
    slot = lax.broadcasted_iota(jnp.int32, (C, ncols), 0)
    pick = (lax.broadcasted_iota(jnp.int32, (C, ncols), 1) == rem_y + 3 * slot).astype(F32).astype(BF16)
    pick = jnp.concatenate([pick, pick], axis=1)
    first = up_third(ox + nest_rows * tile) * 3 - ox - nest_rows * tile
    for s in range(FB_SLOTS):
        r = jnp.minimum(first + 3 * s, rows - 1)
        upper = source[jnp.maximum(r - 1, 0)]
        if s == 0:
            upper = jnp.where(r == 0, above, upper)
        value = advanced(source[r], upper, start[r, 0:1, :])
        fb[s] = jnp.dot(pick, jnp.concatenate(split(value), axis=0), preferred_element_type=F32)


def combine_kernel(nest_rows, pos, e0, e1, e2, e3, out):
    tile = lax.axis_index("tiles")
    my_y, my_z = lax.div(tile, jnp.int32(SIDE)), lax.rem(tile, jnp.int32(SIDE))
    ox = pos[0, 0]
    base = up_third(ox + SIDE * nest_rows * my_y)
    for r in range(FB_GROUP):
        out[r] = jnp.zeros(out.shape[1:], F32)
    for k, ref in enumerate((e0, e1, e2, e3)):
        origin = ox + nest_rows * (SIDE * my_y + wrap(my_z - k))
        row = up_third(origin)
        for s in range(FB_SLOTS):

            @pl.when(3 * (row + s) - origin < nest_rows + STEPS)
            def _(ref=ref, row=row, s=s):
                out[row + s - base] += ref[DEV_ROWS + s]


def window(pos, tile_rows, tile_cols, total):
    ox, oy = pos[0, 0], pos[0, 1]
    first_row = lax.axis_index("tiles") * tile_rows
    low_row, high_row = up_third(ox), third(ox + total - 1)
    owns = (high_row >= first_row) & (low_row < first_row + tile_rows)
    begin = jnp.clip(low_row - first_row, 0, tile_rows - FB_WINDOW)
    corner = third(oy) - lax.axis_index("nests") * tile_cols
    aligned = pl.multiple_of(lax.div(corner, jnp.int32(8)) * 8, 8)
    shift = corner - aligned + up_third(oy) - third(oy)
    return owns, first_row, begin, aligned, shift, up_third(oy) * 3 - oy


def own_kernel(tile_rows, tile_cols, total, pos, parent, from_up, nest_mix, courant, out, buf, parts, sems):
    owns, first_row, begin, aligned, shift, rem_y = window(pos, tile_rows, tile_cols, total)
    ox = pos[0, 0]
    width = buf.shape[2]

    @pl.when(owns)
    def _():
        cols = pl.ds(aligned, WIDE)
        main = pltpu.make_async_copy(
            parent.at[pl.ds(begin, FB_WINDOW), cols], buf.at[pl.ds(1, FB_WINDOW), pl.ds(8, WIDE)], sems.at[0]
        )
        edge = pltpu.make_async_copy(
            parent.at[jnp.maximum(begin - 1, 0), cols], buf.at[0, pl.ds(8, WIDE)], sems.at[1]
        )
        main.start()
        edge.start()
        buf[:, 0:8, :] = jnp.zeros((FB_WINDOW + 1, 8, width), F32)

        c0, c1 = courant[0:1, :], courant[1:2, :]
        diagonal = eye(width)
        r0 = jnp.sum(jnp.where(diagonal, c0, 0.0), axis=1, keepdims=True)
        r1 = jnp.sum(jnp.where(diagonal, c1, 0.0), axis=1, keepdims=True)
        one = nest_mix[...] + jnp.where(diagonal, 1.0 - c0 - c1, 0.0)
        weights = wide_weights(one)
        many = mix(jnp.concatenate([one, one * c0, one * c1], axis=0), weights)
        two, by0, by1 = many[:width], many[width : 2 * width], many[2 * width :]
        paths = {
            (0, 0): mix(two, weights),
            (1, 0): r0 * two + by0 + two * c0,
            (0, 1): r1 * two + by1 + two * c1,
            (2, 0): (r0 * r0) * one + (r0 * one) * c0 + one * (c0 * c0),
            (0, 2): (r1 * r1) * one + (r1 * one) * c1 + one * (c1 * c1),
            (1, 1): (2.0 * r0 * r1) * one + (r0 * one) * c1 + (r1 * one) * c0 + one * (2.0 * c0 * c1),
            (3, 0): jnp.where(diagonal, c0 * c0 * c0, 0.0),
            (0, 3): jnp.where(diagonal, c1 * c1 * c1, 0.0),
            (2, 1): jnp.where(diagonal, 3.0 * c0 * c0 * c1, 0.0),
            (1, 2): jnp.where(diagonal, 3.0 * c0 * c1 * c1, 0.0),
        }

        def corner(low_row, low_col):
            sum_of = jnp.zeros((width, width), F32)
            for (i, j), path in paths.items():
                weight = (i if low_row else 3 - i) * (j if low_col else 3 - j) * (0.5 / 9.0)
                if weight:
                    sum_of = sum_of + weight * path
            return wide_weights(sum_of)

        this_row = jnp.concatenate([corner(False, False), corner(False, True)], axis=0)
        row_before = jnp.concatenate([corner(True, False), corner(True, True)], axis=0)

        main.wait()
        edge.wait()

        @pl.when(begin == 0)
        def _():
            buf[0, pl.ds(8, WIDE), :] = from_up[pl.ds(aligned, WIDE), :]

        for w in range(FB_WINDOW + 1):
            near = buf[w, pl.ds(8 + shift, C), :]
            back = buf[w, pl.ds(7 + shift, C), :]
            parts[w] = jnp.concatenate(split(near) + split(back), axis=1)
        batch = FB_WINDOW // 2
        for w in range(0, FB_WINDOW, batch):
            this = parts[w + 1 : w + 1 + batch].reshape(batch * C, 4 * width)
            before = parts[w : w + batch].reshape(batch * C, 4 * width)
            both = jnp.dot(this, this_row, preferred_element_type=F32) + jnp.dot(
                before, row_before, preferred_element_type=F32
            )
            out[w : w + batch] = (both[:, :width] + both[:, width:]).reshape(batch, C, width)

        first = up_third(ox) - first_row - begin
        at = jnp.clip(first, 0, FB_WINDOW - 1)
        pad = jnp.zeros((24 - FB_WINDOW, width), F32)

        def gather(k, offset):
            column = buf[pl.ds(k, FB_WINDOW), pl.ds(offset + shift, 1), :].reshape(FB_WINDOW, width)
            return jnp.concatenate([buf[at + k, pl.ds(offset + shift, C), :], column, pad], axis=0)

        near = [gather(k, 8) for k in range(2)]
        back = [gather(k, 7) for k in range(2)]
        line = lax.broadcasted_iota(jnp.int32, near[0].shape, 0)
        in_row = line < C
        x = 3 * (first_row + begin + jnp.where(in_row, at, line - C)) - ox
        y = rem_y + 3 * jnp.where(in_row, line, 0)
        start = {}
        for i in range(STEPS + 1):
            lean = jnp.minimum(x, i).astype(F32) * (0.5 / 9.0)
            rest = 0.5 / 3.0 - lean
            right = rest * near[1] + lean * near[0]
            left = rest * back[1] + lean * back[0]
            for j in range(STEPS + 1 - i):
                tilt = jnp.minimum(y, j).astype(F32)
                start[i, j] = right * (3.0 - tilt) + left * tilt
        cells = start
        size = C + 24
        for step in range(STEPS):
            keys = [(i, j) for i in range(STEPS - step) for j in range(STEPS - step - i)]
            mixed = mix(jnp.concatenate([cells[key] for key in keys], axis=0), weights)
            fresh = {}
            for n, (i, j) in enumerate(keys):
                value = mixed[n * size : (n + 1) * size] + c0 * cells[i + 1, j] + c1 * cells[i, j + 1]
                fresh[i, j] = jnp.where((x < i) | (y < j), start[i, j], value)
            cells = fresh
        edges = cells[0, 0]

        @pl.when((first >= 0) & (first < FB_WINDOW))
        def _():
            out[at] = edges[:C]

        for w in range(FB_WINDOW):
            out[w, 0:1, :] = edges[C + w : C + w + 1]


def patch_kernel(tile_rows, tile_cols, nest_rows, ncols, pos, parent, own, kept, g0, g1, g2, g3, out, buf, sems):
    total = nest_rows * SIDE * SIDE
    owns, first_row, begin, aligned, shift, rem_y = window(pos, tile_rows, tile_cols, total)
    my_y = lax.div(lax.axis_index("tiles"), jnp.int32(SIDE))
    ox = pos[0, 0]
    span = SIDE * nest_rows

    @pl.when(owns)
    def _():
        place = (pl.ds(begin, FB_WINDOW), pl.ds(aligned, WIDE))
        buf[...] = kept[...]
        live = rem_y + 3 * lax.broadcasted_iota(jnp.int32, (C, buf.shape[2]), 0) < ncols

        @pl.loop(0, FB_WINDOW)
        def _(w):
            row = first_row + begin + w
            x = 3 * row - ox

            @pl.when((x >= 0) & (x < total))
            def _():
                def from_group(group):
                    r = jnp.clip(row - up_third(ox + span * group), 0, FB_GROUP - 1)
                    return choose(wrap(my_y - group), [ref[r] for ref in (g0, g1, g2, g3)])

                group = lax.div(x, jnp.int32(span))
                value = own[w] + from_group(group)
                spilt = (group > 0) & (x - span * group < STEPS)
                value = value + jnp.where(spilt, from_group(jnp.maximum(group - 1, 0)), 0.0)
                old = buf[w, pl.ds(shift, C), :]
                buf[w, pl.ds(shift, C), :] = jnp.where(live, 0.5 * (old + value), old)

        back = pltpu.make_async_copy(buf, out.at[place], sems.at[0])
        back.start()
        back.wait()


def parent_kernel(
    rows, total, tiles, lines, pos, parent, from_up, from_down, west, east, parent_mix, out, kept, token, done, weights, out_sems
):
    height, cols = parent.shape[0], parent.shape[1]
    count, slots = height // rows, done.shape[0]
    owns, _, begin, aligned, _, _ = window(pos, height, cols, total)
    tile, line = lax.axis_index("tiles"), lax.axis_index("nests")

    def store(i):
        slot = lax.rem(i, slots)
        return pltpu.make_async_copy(done.at[slot], out.at[pl.ds(i * rows, rows)], out_sems.at[slot])

    size = parent_mix.shape[0]
    weights[...] = wide_weights(parent_mix[...] + jnp.where(eye(size), 1.0 - 4.0 * KAPPA, 0.0))
    index = lax.broadcasted_iota(jnp.int32, (cols, size), 0)
    low_edge, high_edge = index == 0, index == cols - 1

    @pl.loop(0, count)
    def _(i):
        @pl.when(i >= slots)
        def _():
            store(i - slots).wait()

        slot = lax.rem(i, slots)
        for r in range(rows):
            at = i * rows + r
            value = parent[at]
            upper = parent[at - 1] if r else jnp.where(i == 0, jnp.where(tile > 0, from_up[...], 0.0), parent[jnp.maximum(at - 1, 0)])
            if r < rows - 1:
                lower = parent[at + 1]
            else:
                lower = jnp.where(
                    i == count - 1, jnp.where(tile < tiles - 1, from_down[...], 0.0), parent[jnp.minimum(at + 1, height - 1)]
                )
            left = jnp.where(low_edge, jnp.where(line > 0, west[pl.ds(at, 1), :], 0.0), pltpu.roll(value, 1, 0))
            right = jnp.where(
                high_edge, jnp.where(line < lines - 1, east[pl.ds(at, 1), :], 0.0), pltpu.roll(value, cols - 1, 0)
            )
            done[slot, r] = mix(value, weights[...]) + KAPPA * ((upper + lower) + (left + right))
        store(i).start()

        @pl.when(owns & (i * rows < begin + FB_WINDOW) & (i * rows + rows > begin))
        def _():
            for r in range(rows):
                at = i * rows + r - begin

                @pl.when((at >= 0) & (at < FB_WINDOW))
                def _(r=r, at=at):
                    kept[at] = done[slot, r, pl.ds(aligned, WIDE), :]

    for k in range(slots):
        store(count - slots + k).wait()
    token[...] = jnp.zeros(token.shape, F32)


def smem():
    return pl.BlockSpec(memory_space=pltpu.SMEM)


def vmem():
    return pl.BlockSpec(memory_space=pltpu.VMEM)


def hbm():
    return pl.BlockSpec(memory_space=pltpu.HBM)


def run(name, kernel, ins, outs, scratch=(), after=(), room=44, flops=0, moved=1, **options):
    given, held = len(ins), len(after)

    def body(*refs):
        kernel(*refs[:given], *refs[given + held :])

    return pl.pallas_call(
        body,
        out_shape=[shape for _, shape in outs],
        in_specs=[spec for spec, _ in ins] + [pl.BlockSpec(memory_space=pl.ANY)] * held,
        out_specs=[spec for spec, _ in outs],
        scratch_shapes=list(scratch),
        compiler_params=pltpu.CompilerParams(vmem_limit_bytes=room << 20),
        cost_estimate=pl.CostEstimate(flops=flops, bytes_accessed=moved << 20, transcendentals=0),
        name=name,
        **options,
    )(*[value for _, value in ins], *after)


def around(count, step):
    return [(i, (i + step) % count) for i in range(count)]


def y_route(k):
    return [(t, (t + SIDE * k) % (SIDE * SIDE)) for t in range(SIDE * SIDE)]


def z_route(k):
    return [(t, t // SIDE * SIDE + (t + k) % SIDE) for t in range(SIDE * SIDE)]


def shards(parent, nest_state, parent_mix, nest_mix, courant, nest_pos):
    tile_rows, tile_cols, width = parent.shape
    state = nest_state[0]
    nest_rows, ncols, _ = state.shape
    total = nest_rows * SIDE * SIDE
    count = SIDE * SIDE
    lines = lax.axis_size("nests")
    S, V, H = smem(), vmem(), hbm()
    big, mid = 52, 44

    def f(*shape):
        return jax.ShapeDtypeStruct(shape, F32)

    def on_tiles(block, route):
        return lax.ppermute(block, "tiles", route)

    packed = run(
        "pack",
        functools.partial(pack_kernel, tile_rows, tile_cols, nest_rows),
        [(S, nest_pos), (H, parent)],
        [(V, f(GROUP_ROWS, C, width))] * SIDE
        + [(V, f(tile_rows, width))] * 2
        + [(V, f(tile_cols, width))] * 2,
        [
            pltpu.VMEM((SIDE, GROUP_ROWS, WIDE, width), F32),
            pltpu.VMEM((2, tile_rows, 8, width), F32),
            pltpu.SemaphoreType.DMA((8,)),
        ],
        room=big,
        flops=1 << 34,
        moved=64,
    )
    b, (west_out, east_out, down_out, up_out) = packed[:4], packed[4:]
    got = {k: on_tiles(b[k], y_route(k)) for k in (1, 3, 2)}
    from_up = on_tiles(down_out, around(count, 1))
    from_down = on_tiles(up_out, around(count, -1))

    fed, tail, mix_kept = run(
        "feed",
        feed_kernel,
        [(S, nest_pos), (V, state), (V, nest_mix), (V, courant)],
        [(V, f(FB_SLOTS, C, width)), (V, f(STEPS, ncols, width)), (V, f(width, width))],
        [
            pltpu.VMEM((nest_rows + STEPS, ncols, width), F32),
            pltpu.VMEM((STEPS - 1, nest_rows + STEPS, ncols, width), F32),
        ],
        after=[west_out],
        flops=1 << 28,
        moved=4,
    )
    west = lax.ppermute(east_out, "nests", around(lines, 1))
    east = lax.ppermute(west_out, "nests", around(lines, -1))
    picked = run(
        "pick",
        functools.partial(pick_kernel, tile_rows, nest_rows),
        [(S, nest_pos)] + [(V, x) for x in (fed, b[0], got[1], got[2], got[3])],
        [(V, f(DEV_ROWS + FB_SLOTS, C, width))] * SIDE,
        after=[west, east, from_down],
    )
    mine = {k: on_tiles(picked[k], z_route(k)) for k in (1, 3, 2)}
    tail, _ = lax.optimization_barrier((tail, picked[1]))
    tail_in = on_tiles(tail, around(count, 1))

    (own,) = run(
        "own_feed",
        functools.partial(own_kernel, tile_rows, tile_cols, total),
        [(S, nest_pos), (H, parent), (V, from_up), (V, mix_kept), (V, courant)],
        [(V, f(FB_WINDOW, C, width))],
        [
            pltpu.VMEM((FB_WINDOW + 1, WIDE + 8, width), F32),
            pltpu.VMEM((FB_WINDOW + 1, C, 4 * width), BF16),
            pltpu.SemaphoreType.DMA((2,)),
        ],
        after=[picked[0]],
        flops=1 << 30,
        moved=8,
    )
    rows = 8
    parent_new, kept, token = run(
        "parent_step",
        functools.partial(parent_kernel, rows, total, count, lines),
        [(S, nest_pos), (V, parent)] + [(V, x) for x in (from_up, from_down, west, east, parent_mix)],
        [(H, f(tile_rows, tile_cols, width)), (V, f(FB_WINDOW, WIDE, width)), (V, f(8, width))],
        [
            pltpu.VMEM((4, rows, tile_cols, width), F32),
            pltpu.VMEM((2 * width, 2 * width), BF16),
            pltpu.SemaphoreType.DMA((4,)),
        ],
        after=[own],
        room=mid,
        flops=2 * tile_rows * tile_cols * 256 * 256,
        moved=10,
    )
    (joined,) = run(
        "combine",
        functools.partial(combine_kernel, nest_rows),
        [(S, nest_pos), (V, picked[0])] + [(V, mine[k]) for k in (1, 2, 3)],
        [(V, f(FB_GROUP, C, width))],
        after=[token],
    )
    groups = {k: on_tiles(joined, y_route(k)) for k in (1, 3, 2)}

    nest_out, moved_on = run(
        "nest_steps",
        functools.partial(nest_kernel, tile_rows, tile_cols),
        [(S, nest_pos), (V, picked[0])]
        + [(V, mine[k]) for k in (1, 2, 3)]
        + [(V, x) for x in (state, tail_in, mix_kept, courant)],
        [(V, f(nest_rows, ncols, width)), (V, f(8, width))],
        [
            pltpu.VMEM((DEV_ROWS, ncols, width), F32),
            pltpu.VMEM((nest_rows + STEPS, ncols, width), F32),
            pltpu.VMEM((STEPS - 1, nest_rows + STEPS, ncols, width), F32),
        ],
        after=[joined],
        flops=1 << 28,
        moved=6,
    )
    (parent_out,) = run(
        "patch",
        functools.partial(patch_kernel, tile_rows, tile_cols, nest_rows, ncols),
        [(S, nest_pos), (H, parent_new), (V, own), (V, kept), (V, joined)] + [(V, groups[k]) for k in (1, 2, 3)],
        [(H, f(tile_rows, tile_cols, width))],
        [pltpu.VMEM((FB_WINDOW, WIDE, width), F32), pltpu.SemaphoreType.DMA((1,))],
        room=big,
        moved=2,
        input_output_aliases={1: 0},
    )
    return parent_out, nest_out[None]


def solution(mesh):
    placed = (
        P("tiles", "nests", None),
        P("nests", "tiles", None, None),
        P(),
        P(),
        P(),
        P("nests", None),
    )
    return jax.shard_map(
        shards,
        mesh=mesh,
        in_specs=placed,
        out_specs=(P("tiles", "nests", None), P("nests", "tiles", None, None)),
        check_vma=False,
    )
```

```python
import functools

import jax
import jax.numpy as jnp
from jax import lax
from jax.experimental import pallas as pl
from jax.experimental.pallas import tpu as pltpu
from jax.sharding import PartitionSpec as P

STEPS = 3
KAPPA = 0.125
C = 48
WIDE = 56
SIDE = 4
GROUP_ROWS = 8
DEV_ROWS = 4
FB_SLOTS = 3
FB_GROUP = 7
FB_WINDOW = 22
F32 = jnp.float32
BF16 = jnp.bfloat16


def third(value):
    return lax.div(value, jnp.int32(3))


def wrap(value):
    return lax.rem(value + 2 * SIDE, jnp.int32(SIDE))


def split(value):
    high = value.astype(BF16)
    return high, (value - high.astype(F32)).astype(BF16)


def wide_weights(matrix):
    high, low = split(matrix)
    row = jnp.concatenate([high, low], axis=1)
    return jnp.concatenate([row, row], axis=0)


def mix(value, weights):
    lhs = jnp.concatenate(split(value), axis=1)
    both = jnp.dot(lhs, weights, preferred_element_type=F32)
    half = both.shape[1] // 2
    return both[:, :half] + both[:, half:]


def choose(way, values):
    result = values[-1]
    for k in range(len(values) - 2, -1, -1):
        result = jnp.where(way == k, values[k], result)
    return result


def eye(size):
    shape = (size, size)
    return lax.broadcasted_iota(jnp.int32, shape, 0) == lax.broadcasted_iota(jnp.int32, shape, 1)


def nest_weights(nest_mix, courant):
    c0, c1 = courant[0:1, :], courant[1:2, :]
    stay = jnp.where(eye(nest_mix.shape[0]), 1.0 - c0 - c1, 0.0)
    return c0, c1, wide_weights(nest_mix[...] + stay)


def owner_place(row, first, tile_rows):
    owner = lax.div(jnp.maximum(row, 0), jnp.int32(tile_rows))
    base = owner * tile_rows
    begin = jnp.clip(first - base, 0, tile_rows - GROUP_ROWS)
    return owner, jnp.clip(row - base - begin, 0, GROUP_ROWS - 1)


def pack_kernel(tile_rows, tile_cols, nest_rows, pos, parent, b0, b1, b2, b3, west, east, down, up, band, cols, sems):
    tile = lax.axis_index("tiles")
    line = lax.axis_index("nests")
    my_y = lax.div(tile, jnp.int32(SIDE))
    corner = third(pos[0, 1]) - line * tile_cols
    aligned = pl.multiple_of(lax.div(corner, jnp.int32(8)) * 8, 8)
    shift = corner - aligned
    copies = []
    for k in range(SIDE):
        group = wrap(my_y + k)
        first = third(pos[0, 0] + SIDE * nest_rows * group) - 1
        begin = jnp.clip(first - tile * tile_rows, 0, tile_rows - GROUP_ROWS)
        copies.append(
            pltpu.make_async_copy(
                parent.at[pl.ds(begin, GROUP_ROWS), pl.ds(aligned, WIDE)], band.at[k], sems.at[k]
            )
        )
    others = [
        pltpu.make_async_copy(parent.at[:, pl.ds(0, 8)], cols.at[0], sems.at[4]),
        pltpu.make_async_copy(parent.at[:, pl.ds(tile_cols - 8, 8)], cols.at[1], sems.at[5]),
        pltpu.make_async_copy(parent.at[tile_rows - 1], down, sems.at[6]),
        pltpu.make_async_copy(parent.at[0], up, sems.at[7]),
    ]
    for copy in copies + others:
        copy.start()
    for k, out in enumerate((b0, b1, b2, b3)):
        copies[k].wait()
        for r in range(GROUP_ROWS):
            out[r] = band[k, r, pl.ds(shift, C), :]
    others[0].wait()
    west[...] = cols[0, :, 0, :]
    others[1].wait()
    east[...] = cols[1, :, 7, :]
    for copy in others[2:]:
        copy.wait()


def pick_kernel(tile_rows, nest_rows, pos, fed, r0, r1, r2, r3, o0, o1, o2, o3):
    tile = lax.axis_index("tiles")
    my_y, my_z = lax.div(tile, jnp.int32(SIDE)), lax.rem(tile, jnp.int32(SIDE))
    first = third(pos[0, 0] + SIDE * nest_rows * my_y) - 1
    for k, out in enumerate((o0, o1, o2, o3)):
        target = my_y * SIDE + wrap(my_z + k)
        top = third(pos[0, 0] + nest_rows * target) - 1
        for j in range(DEV_ROWS):
            owner, place = owner_place(top + j, first, tile_rows)
            way = wrap(my_y - lax.div(owner, jnp.int32(SIDE)))
            out[j] = choose(way, [ref[place] for ref in (r0, r1, r2, r3)])
        for s in range(FB_SLOTS):
            out[DEV_ROWS + s] = fed[s]


def nest_kernel(tile_rows, tile_cols, pos, r0, r1, r2, r3, state, tail, nest_mix, courant, out, token, lines, start, cur):
    tile = lax.axis_index("tiles")
    my_y, my_z = lax.div(tile, jnp.int32(SIDE)), lax.rem(tile, jnp.int32(SIDE))
    nest_rows, ncols, width = state.shape
    halo = STEPS
    ox, oy = pos[0, 0], pos[0, 1]
    phase = lax.rem(oy, jnp.int32(3))
    top = third(ox + nest_rows * tile) - 1
    spot = lax.broadcasted_iota(jnp.int32, (ncols, C), 0) + phase
    near = third(spot)
    frac = spot - 3 * near
    place = lax.broadcasted_iota(jnp.int32, (ncols, C), 1)
    table = jnp.where(place == near, 3 - frac, jnp.where(place == near + 1, frac, 0))
    table = table.astype(F32).astype(BF16)
    for j in range(DEV_ROWS):
        owner = lax.div(jnp.maximum(top + j, 0), jnp.int32(tile_rows))
        way = wrap(my_z - lax.rem(owner, jnp.int32(SIDE)))
        high, low = split(choose(way, [ref[j] for ref in (r0, r1, r2, r3)]))
        lines[j] = jnp.dot(table, high, preferred_element_type=F32) + jnp.dot(
            table, low, preferred_element_type=F32
        )
    for x in range(-halo, nest_rows):
        at = ox + nest_rows * tile + x
        at = jnp.maximum(at, 0)
        near_row = jnp.clip(third(at) - top, 0, DEV_ROWS - 2)
        part = lax.rem(at, jnp.int32(3)).astype(F32)
        interp = (3.0 - part) * lines[near_row] + part * lines[near_row + 1]
        own = state[x] if x >= 0 else tail[x + halo]
        start[x + halo] = 0.5 * (own + interp * (1.0 / 9.0))
    first = tile == 0

    @pl.when(first)
    def _():
        for x in range(halo):
            start[x] = start[halo]

    c0, c1, weights = nest_weights(nest_mix, courant)
    edge_row = lax.broadcasted_iota(jnp.int32, (ncols, width), 0) == 0
    source = start
    for step in range(STEPS):
        last = step == STEPS - 1
        for r in range(nest_rows + halo - 1, step, -1):
            value = source[r]
            left = jnp.where(edge_row, start[r, 0:1, :], pltpu.roll(value, 1, 0))
            value = mix(value, weights) + c0 * source[r - 1] + c1 * left
            if r < halo:
                value = jnp.where(first, start[halo], value)
            if last:
                out[r - halo] = value
            else:
                cur[step, r] = value
        source = cur.at[step]
    token[...] = jnp.zeros(token.shape, F32)


def up_third(value):
    return third(value + 2)


def feed_kernel(pos, state, nest_mix, courant, fb, tail, mix_out, start, cur):
    tile = lax.axis_index("tiles")
    nest_rows, ncols, width = state.shape
    rows = nest_rows + STEPS
    ox, oy = pos[0, 0], pos[0, 1]
    tail[...] = state[nest_rows - STEPS :]
    mix_out[...] = nest_mix[...]
    for x in range(rows):
        start[x] = 0.5 * state[x] if x < nest_rows else jnp.zeros((ncols, width), F32)
    above = jnp.where(tile == 0, start[0], 0.0)
    c0, c1, weights = nest_weights(nest_mix, courant)
    edge_row = lax.broadcasted_iota(jnp.int32, (ncols, width), 0) == 0

    def advanced(value, upper, edge):
        left = jnp.where(edge_row, edge, pltpu.roll(value, 1, 0))
        return mix(value, weights) + c0 * upper + c1 * left

    source = start
    for step in range(STEPS - 1):
        for r in range(nest_rows + step + 1):
            upper = above if r == 0 else source[r - 1]
            cur[step, r] = advanced(source[r], upper, start[r, 0:1, :])
        for r in range(nest_rows + step + 1, rows):
            cur[step, r] = jnp.zeros((ncols, width), F32)
        source = cur.at[step]
    rem_y = lax.rem(3 - lax.rem(oy, jnp.int32(3)), jnp.int32(3))
    slot = lax.broadcasted_iota(jnp.int32, (C, ncols), 0)
    pick = (lax.broadcasted_iota(jnp.int32, (C, ncols), 1) == rem_y + 3 * slot).astype(F32).astype(BF16)
    pick = jnp.concatenate([pick, pick], axis=1)
    first = up_third(ox + nest_rows * tile) * 3 - ox - nest_rows * tile
    for s in range(FB_SLOTS):
        r = jnp.minimum(first + 3 * s, rows - 1)
        upper = source[jnp.maximum(r - 1, 0)]
        if s == 0:
            upper = jnp.where(r == 0, above, upper)
        value = advanced(source[r], upper, start[r, 0:1, :])
        fb[s] = jnp.dot(pick, jnp.concatenate(split(value), axis=0), preferred_element_type=F32)


def combine_kernel(nest_rows, pos, e0, e1, e2, e3, out):
    tile = lax.axis_index("tiles")
    my_y, my_z = lax.div(tile, jnp.int32(SIDE)), lax.rem(tile, jnp.int32(SIDE))
    ox = pos[0, 0]
    base = up_third(ox + SIDE * nest_rows * my_y)
    for r in range(FB_GROUP):
        out[r] = jnp.zeros(out.shape[1:], F32)
    for k, ref in enumerate((e0, e1, e2, e3)):
        origin = ox + nest_rows * (SIDE * my_y + wrap(my_z - k))
        row = up_third(origin)
        for s in range(FB_SLOTS):

            @pl.when(3 * (row + s) - origin < nest_rows + STEPS)
            def _(ref=ref, row=row, s=s):
                out[row + s - base] += ref[DEV_ROWS + s]


def window(pos, tile_rows, tile_cols, total):
    ox, oy = pos[0, 0], pos[0, 1]
    first_row = lax.axis_index("tiles") * tile_rows
    low_row, high_row = up_third(ox), third(ox + total - 1)
    owns = (high_row >= first_row) & (low_row < first_row + tile_rows)
    begin = jnp.clip(low_row - first_row, 0, tile_rows - FB_WINDOW)
    corner = third(oy) - lax.axis_index("nests") * tile_cols
    aligned = pl.multiple_of(lax.div(corner, jnp.int32(8)) * 8, 8)
    shift = corner - aligned + up_third(oy) - third(oy)
    return owns, first_row, begin, aligned, shift, up_third(oy) * 3 - oy


def own_kernel(tile_rows, tile_cols, total, pos, parent, from_up, nest_mix, courant, out, buf, parts, sems):
    owns, first_row, begin, aligned, shift, rem_y = window(pos, tile_rows, tile_cols, total)
    ox = pos[0, 0]
    width = buf.shape[2]

    @pl.when(owns)
    def _():
        cols = pl.ds(aligned, WIDE)
        main = pltpu.make_async_copy(
            parent.at[pl.ds(begin, FB_WINDOW), cols], buf.at[pl.ds(1, FB_WINDOW), pl.ds(8, WIDE)], sems.at[0]
        )
        edge = pltpu.make_async_copy(
            parent.at[jnp.maximum(begin - 1, 0), cols], buf.at[0, pl.ds(8, WIDE)], sems.at[1]
        )
        main.start()
        edge.start()
        buf[:, 0:8, :] = jnp.zeros((FB_WINDOW + 1, 8, width), F32)

        c0, c1 = courant[0:1, :], courant[1:2, :]
        diagonal = eye(width)
        r0 = jnp.sum(jnp.where(diagonal, c0, 0.0), axis=1, keepdims=True)
        r1 = jnp.sum(jnp.where(diagonal, c1, 0.0), axis=1, keepdims=True)
        one = nest_mix[...] + jnp.where(diagonal, 1.0 - c0 - c1, 0.0)
        weights = wide_weights(one)
        many = mix(jnp.concatenate([one, one * c0, one * c1], axis=0), weights)
        two, by0, by1 = many[:width], many[width : 2 * width], many[2 * width :]
        paths = {
            (0, 0): mix(two, weights),
            (1, 0): r0 * two + by0 + two * c0,
            (0, 1): r1 * two + by1 + two * c1,
            (2, 0): (r0 * r0) * one + (r0 * one) * c0 + one * (c0 * c0),
            (0, 2): (r1 * r1) * one + (r1 * one) * c1 + one * (c1 * c1),
            (1, 1): (2.0 * r0 * r1) * one + (r0 * one) * c1 + (r1 * one) * c0 + one * (2.0 * c0 * c1),
            (3, 0): jnp.where(diagonal, c0 * c0 * c0, 0.0),
            (0, 3): jnp.where(diagonal, c1 * c1 * c1, 0.0),
            (2, 1): jnp.where(diagonal, 3.0 * c0 * c0 * c1, 0.0),
            (1, 2): jnp.where(diagonal, 3.0 * c0 * c1 * c1, 0.0),
        }

        def corner(low_row, low_col):
            sum_of = jnp.zeros((width, width), F32)
            for (i, j), path in paths.items():
                weight = (i if low_row else 3 - i) * (j if low_col else 3 - j) * (0.5 / 9.0)
                if weight:
                    sum_of = sum_of + weight * path
            return wide_weights(sum_of)

        this_row = jnp.concatenate([corner(False, False), corner(False, True)], axis=0)
        row_before = jnp.concatenate([corner(True, False), corner(True, True)], axis=0)

        main.wait()
        edge.wait()

        @pl.when(begin == 0)
        def _():
            buf[0, pl.ds(8, WIDE), :] = from_up[pl.ds(aligned, WIDE), :]

        for w in range(FB_WINDOW + 1):
            near = buf[w, pl.ds(8 + shift, C), :]
            back = buf[w, pl.ds(7 + shift, C), :]
            parts[w] = jnp.concatenate(split(near) + split(back), axis=1)
        batch = FB_WINDOW // 2
        for w in range(0, FB_WINDOW, batch):
            this = parts[w + 1 : w + 1 + batch].reshape(batch * C, 4 * width)
            before = parts[w : w + batch].reshape(batch * C, 4 * width)
            both = jnp.dot(this, this_row, preferred_element_type=F32) + jnp.dot(
                before, row_before, preferred_element_type=F32
            )
            out[w : w + batch] = (both[:, :width] + both[:, width:]).reshape(batch, C, width)

        first = up_third(ox) - first_row - begin
        at = jnp.clip(first, 0, FB_WINDOW - 1)
        pad = jnp.zeros((24 - FB_WINDOW, width), F32)

        def gather(k, offset):
            column = buf[pl.ds(k, FB_WINDOW), pl.ds(offset + shift, 1), :].reshape(FB_WINDOW, width)
            return jnp.concatenate([buf[at + k, pl.ds(offset + shift, C), :], column, pad], axis=0)

        near = [gather(k, 8) for k in range(2)]
        back = [gather(k, 7) for k in range(2)]
        line = lax.broadcasted_iota(jnp.int32, near[0].shape, 0)
        in_row = line < C
        x = 3 * (first_row + begin + jnp.where(in_row, at, line - C)) - ox
        y = rem_y + 3 * jnp.where(in_row, line, 0)
        start = {}
        for i in range(STEPS + 1):
            lean = jnp.minimum(x, i).astype(F32) * (0.5 / 9.0)
            rest = 0.5 / 3.0 - lean
            right = rest * near[1] + lean * near[0]
            left = rest * back[1] + lean * back[0]
            for j in range(STEPS + 1 - i):
                tilt = jnp.minimum(y, j).astype(F32)
                start[i, j] = right * (3.0 - tilt) + left * tilt
        cells = start
        size = C + 24
        for step in range(STEPS):
            keys = [(i, j) for i in range(STEPS - step) for j in range(STEPS - step - i)]
            mixed = mix(jnp.concatenate([cells[key] for key in keys], axis=0), weights)
            fresh = {}
            for n, (i, j) in enumerate(keys):
                value = mixed[n * size : (n + 1) * size] + c0 * cells[i + 1, j] + c1 * cells[i, j + 1]
                fresh[i, j] = jnp.where((x < i) | (y < j), start[i, j], value)
            cells = fresh
        edges = cells[0, 0]

        @pl.when((first >= 0) & (first < FB_WINDOW))
        def _():
            out[at] = edges[:C]

        for w in range(FB_WINDOW):
            out[w, 0:1, :] = edges[C + w : C + w + 1]


def patch_kernel(tile_rows, tile_cols, nest_rows, ncols, pos, parent, own, kept, g0, g1, g2, g3, out, buf, sems):
    total = nest_rows * SIDE * SIDE
    owns, first_row, begin, aligned, shift, rem_y = window(pos, tile_rows, tile_cols, total)
    my_y = lax.div(lax.axis_index("tiles"), jnp.int32(SIDE))
    ox = pos[0, 0]
    span = SIDE * nest_rows

    @pl.when(owns)
    def _():
        half = FB_WINDOW // 2
        y = rem_y + 3 * lax.broadcasted_iota(jnp.int32, (C, buf.shape[2]), 0)
        buf[...] = kept[...]

        def back(part):
            rows = pl.ds(begin + part * half, half)
            return pltpu.make_async_copy(
                buf.at[pl.ds(part * half, half)], out.at[rows, pl.ds(aligned, WIDE)], sems.at[part]
            )

        for w in range(FB_WINDOW):
            row = first_row + begin + w
            x = 3 * row - ox
            limit = jnp.where((x >= 0) & (x < total), ncols, 0)
            x = jnp.clip(x, 0, total - 1)

            def from_group(group, row=row):
                r = jnp.clip(row - up_third(ox + span * group), 0, FB_GROUP - 1)
                return choose(wrap(my_y - group), [ref[r] for ref in (g0, g1, g2, g3)])

            group = lax.div(x, jnp.int32(span))
            value = own[w] + from_group(group)
            spilt = (group > 0) & (x - span * group < STEPS)
            value = value + jnp.where(spilt, from_group(jnp.maximum(group - 1, 0)), 0.0)
            old = kept[w, pl.ds(shift, C), :]
            buf[w, pl.ds(shift, C), :] = jnp.where(y < limit, 0.5 * (old + value), old)
            if w == half - 1:
                back(0).start()
        back(1).start()
        back(0).wait()
        back(1).wait()


def parent_kernel(
    rows, total, tiles, lines, pos, parent, from_up, from_down, west, east, parent_mix, out, kept, token, done, weights, out_sems
):
    height, cols = parent.shape[0], parent.shape[1]
    count, slots = height // rows, done.shape[0]
    owns, _, begin, aligned, _, _ = window(pos, height, cols, total)
    tile, line = lax.axis_index("tiles"), lax.axis_index("nests")

    def store(i):
        slot = lax.rem(i, slots)
        return pltpu.make_async_copy(done.at[slot], out.at[pl.ds(i * rows, rows)], out_sems.at[slot])

    size = parent_mix.shape[0]
    weights[...] = wide_weights(parent_mix[...] + jnp.where(eye(size), 1.0 - 4.0 * KAPPA, 0.0))
    index = lax.broadcasted_iota(jnp.int32, (cols, size), 0)
    low_edge, high_edge = index == 0, index == cols - 1

    @pl.loop(0, count)
    def _(i):
        @pl.when(i >= slots)
        def _():
            store(i - slots).wait()

        slot = lax.rem(i, slots)
        for r in range(rows):
            at = i * rows + r
            value = parent[at]
            upper = parent[at - 1] if r else jnp.where(i == 0, jnp.where(tile > 0, from_up[...], 0.0), parent[jnp.maximum(at - 1, 0)])
            if r < rows - 1:
                lower = parent[at + 1]
            else:
                lower = jnp.where(
                    i == count - 1, jnp.where(tile < tiles - 1, from_down[...], 0.0), parent[jnp.minimum(at + 1, height - 1)]
                )
            left = jnp.where(low_edge, jnp.where(line > 0, west[pl.ds(at, 1), :], 0.0), pltpu.roll(value, 1, 0))
            right = jnp.where(
                high_edge, jnp.where(line < lines - 1, east[pl.ds(at, 1), :], 0.0), pltpu.roll(value, cols - 1, 0)
            )
            done[slot, r] = mix(value, weights[...]) + KAPPA * ((upper + lower) + (left + right))
        store(i).start()

        @pl.when(owns & (i * rows < begin + FB_WINDOW) & (i * rows + rows > begin))
        def _():
            for r in range(rows):
                at = i * rows + r - begin

                @pl.when((at >= 0) & (at < FB_WINDOW))
                def _(r=r, at=at):
                    kept[at] = done[slot, r, pl.ds(aligned, WIDE), :]

    for k in range(slots):
        store(count - slots + k).wait()
    token[...] = jnp.zeros(token.shape, F32)


def smem():
    return pl.BlockSpec(memory_space=pltpu.SMEM)


def vmem():
    return pl.BlockSpec(memory_space=pltpu.VMEM)


def hbm():
    return pl.BlockSpec(memory_space=pltpu.HBM)


def run(name, kernel, ins, outs, scratch=(), after=(), room=44, flops=0, moved=1, **options):
    given, held = len(ins), len(after)

    def body(*refs):
        kernel(*refs[:given], *refs[given + held :])

    return pl.pallas_call(
        body,
        out_shape=[shape for _, shape in outs],
        in_specs=[spec for spec, _ in ins] + [pl.BlockSpec(memory_space=pl.ANY)] * held,
        out_specs=[spec for spec, _ in outs],
        scratch_shapes=list(scratch),
        compiler_params=pltpu.CompilerParams(vmem_limit_bytes=room << 20),
        cost_estimate=pl.CostEstimate(flops=flops, bytes_accessed=moved << 20, transcendentals=0),
        name=name,
        **options,
    )(*[value for _, value in ins], *after)


def around(count, step):
    return [(i, (i + step) % count) for i in range(count)]


def y_route(k):
    return [(t, (t + SIDE * k) % (SIDE * SIDE)) for t in range(SIDE * SIDE)]


def z_route(k):
    return [(t, t // SIDE * SIDE + (t + k) % SIDE) for t in range(SIDE * SIDE)]


def shards(parent, nest_state, parent_mix, nest_mix, courant, nest_pos):
    tile_rows, tile_cols, width = parent.shape
    state = nest_state[0]
    nest_rows, ncols, _ = state.shape
    total = nest_rows * SIDE * SIDE
    count = SIDE * SIDE
    lines = lax.axis_size("nests")
    S, V, H = smem(), vmem(), hbm()
    big, mid = 52, 44

    def f(*shape):
        return jax.ShapeDtypeStruct(shape, F32)

    def on_tiles(block, route):
        return lax.ppermute(block, "tiles", route)

    packed = run(
        "pack",
        functools.partial(pack_kernel, tile_rows, tile_cols, nest_rows),
        [(S, nest_pos), (H, parent)],
        [(V, f(GROUP_ROWS, C, width))] * SIDE
        + [(V, f(tile_rows, width))] * 2
        + [(V, f(tile_cols, width))] * 2,
        [
            pltpu.VMEM((SIDE, GROUP_ROWS, WIDE, width), F32),
            pltpu.VMEM((2, tile_rows, 8, width), F32),
            pltpu.SemaphoreType.DMA((8,)),
        ],
        room=big,
        flops=1 << 34,
        moved=64,
    )
    b, (west_out, east_out, down_out, up_out) = packed[:4], packed[4:]
    got = {k: on_tiles(b[k], y_route(k)) for k in (1, 3, 2)}
    from_up = on_tiles(down_out, around(count, 1))
    from_down = on_tiles(up_out, around(count, -1))

    fed, tail, mix_kept = run(
        "feed",
        feed_kernel,
        [(S, nest_pos), (V, state), (V, nest_mix), (V, courant)],
        [(V, f(FB_SLOTS, C, width)), (V, f(STEPS, ncols, width)), (V, f(width, width))],
        [
            pltpu.VMEM((nest_rows + STEPS, ncols, width), F32),
            pltpu.VMEM((STEPS - 1, nest_rows + STEPS, ncols, width), F32),
        ],
        after=[west_out],
        flops=1 << 28,
        moved=4,
    )
    west = lax.ppermute(east_out, "nests", around(lines, 1))
    east = lax.ppermute(west_out, "nests", around(lines, -1))
    picked = run(
        "pick",
        functools.partial(pick_kernel, tile_rows, nest_rows),
        [(S, nest_pos)] + [(V, x) for x in (fed, b[0], got[1], got[2], got[3])],
        [(V, f(DEV_ROWS + FB_SLOTS, C, width))] * SIDE,
        after=[west, east, from_down],
    )
    mine = {k: on_tiles(picked[k], z_route(k)) for k in (1, 3, 2)}
    tail, _ = lax.optimization_barrier((tail, picked[1]))
    tail_in = on_tiles(tail, around(count, 1))

    (own,) = run(
        "own_feed",
        functools.partial(own_kernel, tile_rows, tile_cols, total),
        [(S, nest_pos), (H, parent), (V, from_up), (V, mix_kept), (V, courant)],
        [(V, f(FB_WINDOW, C, width))],
        [
            pltpu.VMEM((FB_WINDOW + 1, WIDE + 8, width), F32),
            pltpu.VMEM((FB_WINDOW + 1, C, 4 * width), BF16),
            pltpu.SemaphoreType.DMA((2,)),
        ],
        after=[picked[0]],
        flops=1 << 30,
        moved=8,
    )
    rows = 8
    parent_new, kept, token = run(
        "parent_step",
        functools.partial(parent_kernel, rows, total, count, lines),
        [(S, nest_pos), (V, parent)] + [(V, x) for x in (from_up, from_down, west, east, parent_mix)],
        [(H, f(tile_rows, tile_cols, width)), (V, f(FB_WINDOW, WIDE, width)), (V, f(8, width))],
        [
            pltpu.VMEM((4, rows, tile_cols, width), F32),
            pltpu.VMEM((2 * width, 2 * width), BF16),
            pltpu.SemaphoreType.DMA((4,)),
        ],
        after=[own],
        room=mid,
        flops=2 * tile_rows * tile_cols * 256 * 256,
        moved=10,
    )
    (joined,) = run(
        "combine",
        functools.partial(combine_kernel, nest_rows),
        [(S, nest_pos), (V, picked[0])] + [(V, mine[k]) for k in (1, 2, 3)],
        [(V, f(FB_GROUP, C, width))],
        after=[token],
    )
    groups = {k: on_tiles(joined, y_route(k)) for k in (1, 3, 2)}

    nest_out, moved_on = run(
        "nest_steps",
        functools.partial(nest_kernel, tile_rows, tile_cols),
        [(S, nest_pos), (V, picked[0])]
        + [(V, mine[k]) for k in (1, 2, 3)]
        + [(V, x) for x in (state, tail_in, mix_kept, courant)],
        [(V, f(nest_rows, ncols, width)), (V, f(8, width))],
        [
            pltpu.VMEM((DEV_ROWS, ncols, width), F32),
            pltpu.VMEM((nest_rows + STEPS, ncols, width), F32),
            pltpu.VMEM((STEPS - 1, nest_rows + STEPS, ncols, width), F32),
        ],
        after=[joined],
        flops=1 << 28,
        moved=6,
    )
    (parent_out,) = run(
        "patch",
        functools.partial(patch_kernel, tile_rows, tile_cols, nest_rows, ncols),
        [(S, nest_pos), (H, parent_new), (V, own), (V, kept), (V, joined)] + [(V, groups[k]) for k in (1, 2, 3)],
        [(H, f(tile_rows, tile_cols, width))],
        [pltpu.VMEM((FB_WINDOW, WIDE, width), F32), pltpu.SemaphoreType.DMA((2,))],
        room=big,
        moved=2,
        input_output_aliases={1: 0},
    )
    return parent_out, nest_out[None]


def solution(mesh):
    placed = (
        P("tiles", "nests", None),
        P("nests", "tiles", None, None),
        P(),
        P(),
        P(),
        P("nests", None),
    )
    return jax.shard_map(
        shards,
        mesh=mesh,
        in_specs=placed,
        out_specs=(P("tiles", "nests", None), P("nests", "tiles", None, None)),
        check_vma=False,
    )
```
